32 devices in a mesh: lat: 8 (over z, core), lon: 4 (over y, x).
Axes of the slice: x: 2, y: 2, z: 4, core: 2. Of those that a mesh axis runs over, the one named last changes fastest.
Arguments:
- pedersen: float32 [16, 1024, 2048], P(None, 'lat', 'lon'), may hold values from 0.2 to 2
- hall_conductivity: float32 [16, 1024, 2048], P(None, 'lat', 'lon'), may hold values from 0.1 to 1.5
- east_wind: float32 [16, 1024, 2048], P(None, 'lat', 'lon'), may hold values from -6 to 6
- north_wind: float32 [16, 1024, 2048], P(None, 'lat', 'lon'), may hold values from -6 to 6
- ion_density: float32 [3, 1024, 2048], P(None, 'lat', 'lon'), may hold values from 0.5 to 2
Outputs:
- potential: float32 [1024, 2048], P('lat', 'lon')
- ion_update: float32 [3, 1024, 2048], P(None, 'lat', 'lon')
The draws below stay inside these ranges and needn't reach their ends.
All inputs are finite; a program needn't handle non-finite values. Where the reference program divides by a largest or mean magnitude, that divisor is 1e-20 or more.
Results may differ from the reference program's by a relative error of at most 0.00002.
Values sent between devices are 32-bit elements; how exact they have to be, the bound alone decides.
A program may use at most 192 MiB of HBM per device.

```python
import math
import jax
import jax.numpy as jnp
from jax import lax

LEV = 16
SWEEPS = 16
NLAT = 1024
NLON = 2048


def steps_of(own_key, extent, pieces, least, top_value):
    level, own = 1.0, jax.random.fold_in(own_key, 6)
    for axis_at, shards_of in pieces:
        heights = jnp.exp(jax.random.uniform(jax.random.fold_in(own, axis_at), (shards_of,), jnp.float32, least / len(pieces), top_value / len(pieces)))
        level = level * jnp.repeat(heights, extent[axis_at] // shards_of).reshape([-1 if axis == axis_at else 1 for axis in range(len(extent))])
    return level


def bell_draw(rng, extent, scale, bound, split=(), kind=jnp.bfloat16):
    entries = scale * jax.random.normal(rng, extent, jnp.float32)
    if split:
        entries = entries * steps_of(rng, extent, split, -0.22, 0.18)
    return jnp.clip(entries, -bound, bound).astype(kind)


def setup_inputs(seed: int = 0) -> dict:
    key_list = jax.random.split(jax.random.key(seed), 6)
    return {
        "pedersen": jnp.clip(jnp.exp(math.log(2.0) - 2.3025851 * jax.random.uniform(key_list[0], (LEV, NLAT, NLON), jnp.float32) ** steps_of(key_list[0], (LEV, NLAT, NLON), ((1, 8), (2, 4)), -0.2, 0.2)), 0.2, 2.0),
        "hall_conductivity": jnp.clip(jnp.exp(math.log(1.5) - 2.7080502 * jax.random.uniform(key_list[1], (LEV, NLAT, NLON), jnp.float32) ** steps_of(key_list[1], (LEV, NLAT, NLON), ((1, 8), (2, 4)), -0.2, 0.2)), 0.1, 1.5),
        "east_wind": bell_draw(key_list[2], (LEV, NLAT, NLON), 1.0, 6.0, ((1, 8), (2, 4)), jnp.float32),
        "north_wind": bell_draw(key_list[3], (LEV, NLAT, NLON), 1.0, 6.0, ((1, 8), (2, 4)), jnp.float32),
        "ion_density": jnp.clip(jnp.exp(math.log(2.0) - 1.3862944 * jax.random.uniform(key_list[4], (3, NLAT, NLON), jnp.float32) ** steps_of(key_list[4], (3, NLAT, NLON), ((1, 8), (2, 4)), -0.2, 0.2)), 0.5, 2.0),
    }


DAMPING = 0.0001
LOW_BOUND = 0.05
HIGH_BOUND = 2.0
COURANT = 0.8
MOBILITY = (1.0, 0.6, 0.3)
NEIGHBOURS = ((-1, 0, 1.0), (1, 0, 1.0), (0, -1, 1.0), (0, 1, 1.0), (-1, -1, 0.5), (-1, 1, 0.5), (1, -1, 0.5), (1, 1, 0.5))


def thickness():
    levels = jnp.arange(LEV, dtype=jnp.float32)
    return (0.5 + levels / LEV) / LEV


def chebyshev_factors():
    theta = 0.5 * (HIGH_BOUND + LOW_BOUND)
    delta = 0.5 * (HIGH_BOUND - LOW_BOUND)
    sigma_one = theta / delta
    rho_prev = 1.0 / sigma_one
    first_list = []
    second_list = []
    for sweep in range(SWEEPS):
        rho_next = 1.0 / (2.0 * sigma_one - rho_prev)
        first_list.append(rho_next * rho_prev)
        second_list.append(2.0 * rho_next / delta)
        rho_prev = rho_next
    return theta, first_list, second_list


def extend(field, width):
    padded = jnp.pad(field, ((width, width), (0, 0)))
    return jnp.concatenate([padded[:, -width:], padded, padded[:, :width]], axis=1)


def window(array, shift_lat, shift_lon):
    height = array.shape[0] - 2
    breadth = array.shape[1] - 2
    return array[1 + shift_lat:1 + shift_lat + height, 1 + shift_lon:1 + shift_lon + breadth]


def stencil(sigma_ext):
    center = window(sigma_ext, 0, 0)
    weights = []
    diagonal = jnp.zeros_like(center) + DAMPING
    for shift_lat, shift_lon, factor in NEIGHBOURS:
        weight = factor * 0.5 * (center + window(sigma_ext, shift_lat, shift_lon))
        weights.append(weight)
    for weight in weights:
        diagonal = diagonal + weight
    return weights, diagonal


def apply_operator(field_ext, weights, diagonal):
    result = diagonal * window(field_ext, 0, 0)
    for index_pair, (shift_lat, shift_lon, factor) in enumerate(NEIGHBOURS):
        result = result - weights[index_pair] * window(field_ext, shift_lat, shift_lon)
    return result


def divergence(east_ext, north_ext):
    return 0.5 * (window(east_ext, 0, 1) - window(east_ext, 0, -1)) + 0.5 * (window(north_ext, 1, 0) - window(north_ext, -1, 0))


def advect(density_ext, cross_east, cross_north):
    density = window(density_ext, 0, 0)
    result = density - jnp.maximum(cross_east, 0.0) * (density - window(density_ext, 0, -1))
    result = result - jnp.minimum(cross_east, 0.0) * (window(density_ext, 0, 1) - density)
    result = result - jnp.maximum(cross_north, 0.0) * (density - window(density_ext, -1, 0))
    result = result - jnp.minimum(cross_north, 0.0) * (window(density_ext, 1, 0) - density)
    return result


def reference(pedersen, hall_conductivity, east_wind, north_wind, ion_density):
    layer = thickness()

    def accumulate(level, totals):
        sigma_p = pedersen[level]
        sigma_h = hall_conductivity[level]
        wind_e = east_wind[level]
        wind_n = north_wind[level]
        return (totals[0] + layer[level] * sigma_p,
                totals[1] + layer[level] * (sigma_p * wind_e + sigma_h * wind_n),
                totals[2] + layer[level] * (sigma_p * wind_n - sigma_h * wind_e))

    zeros = jnp.zeros(pedersen.shape[1:], jnp.float32)
    sigma, current_east, current_north = lax.fori_loop(0, LEV, accumulate, (zeros, zeros, zeros))
    sigma = sigma + sigma[::-1]
    current_east = current_east + current_east[::-1]
    current_north = current_north + current_north[::-1]
    weights, diagonal = stencil(extend(sigma, 1))
    source = divergence(extend(current_east, 1), extend(current_north, 1))
    theta, first_list, second_list = chebyshev_factors()
    solution = jnp.zeros_like(source)
    update = source / diagonal / theta
    for sweep in range(SWEEPS):
        solution = solution + update
        image = apply_operator(extend(solution, 1), weights, diagonal)
        scaled = (source - image) / diagonal
        update = first_list[sweep] * update + second_list[sweep] * scaled
    potential = solution
    potential_ext = extend(potential, 1)
    drift_east = -0.5 * (window(potential_ext, 1, 0) - window(potential_ext, -1, 0))
    drift_north = 0.5 * (window(potential_ext, 0, 1) - window(potential_ext, 0, -1))
    fastest = jnp.max(jnp.abs(drift_east) + jnp.abs(drift_north))
    time_step = COURANT / (fastest + 1e-6)
    results = []
    for species in range(3):
        cross_east = MOBILITY[species] * time_step * drift_east
        cross_north = MOBILITY[species] * time_step * drift_north
        results.append(advect(extend(ion_density[species], 1), cross_east, cross_north))
    return potential, jnp.stack(results)
```

```python
import functools

import jax
import jax.numpy as jnp
from jax import lax
from jax.experimental import pallas as pl
from jax.experimental.pallas import tpu as pltpu
from jax.sharding import PartitionSpec as P

SWEEPS = 16
DAMPING = 0.0001
LOW_BOUND = 0.05
HIGH_BOUND = 2.0
COURANT = 0.8
MOBILITY = (1.0, 0.6, 0.3)
MESH = pl.DeviceIdType.MESH
GUARD = 24
HALO = 16
PIECES = 4
THETA = 0.5 * (HIGH_BOUND + LOW_BOUND)
F32 = jnp.float32
BF16 = jnp.bfloat16


def chebyshev_factors():
    delta = 0.5 * (HIGH_BOUND - LOW_BOUND)
    sigma_one = THETA / delta
    rho_prev = 1.0 / sigma_one
    first_list = []
    second_list = []
    for sweep in range(SWEEPS):
        rho_next = 1.0 / (2.0 * sigma_one - rho_prev)
        first_list.append(rho_next * rho_prev)
        second_list.append(2.0 * rho_next / delta)
        rho_prev = rho_next
    return first_list, second_list


def kernel(
    nlat, nlon, lev, rows, lt,
    ped_h, hall_h, east_h, north_h, ion_h,
    pot_o, upd_o,
    ped, hall, east, north,
    ion, ion_fr, ion_fl, ion_a, ion_b,
    sig, cur_e, cur_n, e_fr, e_fl, s_one, t_out, sig_rx, t_rx,
    S, src, s_fr, s_fl, v_fr, v_fl,
    lhs, to_strided, to_plain, coef,
    SP, U, SR, rR, mR, invR, spR, X, xr, xn, dnb,
    flux, mx, mrx,
    sem_in, sem_ion, ss, rs, ss_max, rs_max,
):
    n_rt = rows // 8
    nt = lt + 1
    width = nt * 128
    R = (rows + 2 * HALO) // 8
    n_dev = nlat * nlon
    me_lat = lax.axis_index("lat")
    me_lon = lax.axis_index("lon")
    has_up = me_lat > 0
    has_dn = me_lat < nlat - 1
    up = (jnp.maximum(me_lat - 1, 0), me_lon)
    dn = (jnp.minimum(me_lat + 1, nlat - 1), me_lon)
    lf = (me_lat, lax.rem(me_lon + nlon - 1, nlon))
    rt = (me_lat, lax.rem(me_lon + 1, nlon))
    mirror = (nlat - 1 - me_lat, me_lon)
    others = [
        (lax.rem(me_lat + a, nlat), lax.rem(me_lon + b, nlon))
        for a in range(nlat) for b in range(nlon) if a or b
    ]

    barrier = pltpu.get_barrier_semaphore()
    for dev in others:
        pl.semaphore_signal(barrier, inc=1, device_id=dev, device_id_type=MESH)

    per = n_rt // PIECES
    piece_order = [0, PIECES - 1] + list(range(1, PIECES - 1))
    hbm_in = (ped_h, hall_h, east_h, north_h)
    vm_in = (ped, hall, east, north)

    def in_copy(a, c):
        row = pl.multiple_of(8 * c, 8)
        return pltpu.make_async_copy(
            hbm_in[a].at[:, pl.ds(row, 8), :], vm_in[a].at[:, pl.ds(row, 8), :], sem_in.at[c, a]
        )

    def ion_copy(s, t):
        return pltpu.make_async_copy(
            ion_h.at[s, :, t * 128 : (t + 1) * 128], ion.at[s, t, 8 : 8 + rows], sem_ion.at[s, t]
        )

    for q in piece_order:
        for c in range(q * per, (q + 1) * per):
            for a in range(4):
                in_copy(a, c).start()
    for s in range(3):
        for t in range(lt):
            ion_copy(s, t).start()

    first_list, second_list = chebyshev_factors()
    for k in range(SWEEPS):
        coef[0, k] = jnp.float32(first_list[k])
        coef[1, k] = jnp.float32(second_list[k])

    counter = [0]

    def rcopy(src_ref, dst_ref, dev):
        k = counter[0]
        counter[0] += 1
        return pltpu.make_async_remote_copy(
            src_ref=src_ref, dst_ref=dst_ref, send_sem=ss.at[k], recv_sem=rs.at[k],
            device_id=dev, device_id_type=MESH,
        )

    lane = lax.broadcasted_iota(jnp.int32, (8, 128), 1)
    sub = lax.broadcasted_iota(jnp.int32, (8, 128), 0)

    def shifts(v):
        m = len(v)
        a = [pltpu.roll(t, 1, 1) for t in v]
        b = [pltpu.roll(t, 127, 1) for t in v]
        left = [jnp.where(lane == 0, a[j - 1], a[j]) for j in range(m)]
        right = [jnp.where(lane == 127, b[(j + 1) % m], b[j]) for j in range(m)]
        return left, right

    def rev8(v):
        v = pltpu.roll(v, 4, 0)
        for b in (2, 1):
            v = jnp.where((sub & b) == 0, pltpu.roll(v, 8 - b, 0), pltpu.roll(v, b, 0))
        return v

    @pl.loop(0, width // 16, unroll=4)
    def _(c):
        row = lax.broadcasted_iota(jnp.int32, (16, 128), 0) + 16 * c
        col = lax.broadcasted_iota(jnp.int32, (16, 128), 1)
        for t in range(nt):
            there = jnp.where(row == col * nt + t, 1.0, 0.0).astype(BF16)
            for part in range(3):
                at = pl.ds(pl.multiple_of(part * width + 16 * c, 16), 16)
                to_strided[at, t * 128 : (t + 1) * 128] = there

    weight = [(0.5 + l / lev) / lev for l in range(lev)]

    def columns(lo, hi):
        @pl.loop(lo, hi)
        def _(c):
            row = pl.multiple_of(8 * c, 8)
            for a in range(4):
                in_copy(a, c).wait()
            for t in range(lt):
                at = (pl.ds(row, 8), slice(t * 128, (t + 1) * 128))
                acc = [jnp.zeros((8, 128), F32)] * 3
                for l in range(lev):
                    p, h = weight[l] * ped[(l,) + at], weight[l] * hall[(l,) + at]
                    e, n = east[(l,) + at], north[(l,) + at]
                    acc = [acc[0] + p, acc[1] + (p * e + h * n), acc[2] + (p * n - h * e)]
                sig[t, pl.ds(row, 8), :] = acc[0]
                cur_e[t, pl.ds(row, 8), :] = acc[1]
                cur_n[t, pl.ds(row + 8, 8), :] = acc[2]

    sig_copies, e_copies = {}, {}
    n_up = rcopy(cur_n.at[:, 8:16], cur_n.at[:, rows + 8 : rows + 16], up)
    n_dn = rcopy(cur_n.at[:, rows : rows + 8], cur_n.at[:, 0:8], dn)
    i_up = rcopy(ion.at[:, :, 8:16], ion.at[:, :, rows + 8 : rows + 16], up)
    i_dn = rcopy(ion.at[:, :, rows : rows + 8], ion.at[:, :, 0:8], dn)
    i_lf = rcopy(ion.at[:, 0, 8 : 8 + rows], ion_fr, lf)
    i_rt = rcopy(ion.at[:, lt - 1, 8 : 8 + rows], ion_fl, rt)

    for i, q in enumerate(piece_order):
        columns(q * per, (q + 1) * per)
        if i == 0:
            pl.semaphore_wait(barrier, n_dev - 1)
        band = slice(q * per * 8, (q + 1) * per * 8)
        sig_copies[q] = rcopy(sig.at[:, band], sig_rx.at[:, band], mirror)
        sig_copies[q].start()
        if q == 0:
            @pl.when(has_up)
            def _():
                n_up.start()
        if q == PIECES - 1:
            @pl.when(has_dn)
            def _():
                n_dn.start()
        e_copies[q] = (
            rcopy(cur_e.at[0, band], e_fr.at[band], lf),
            rcopy(cur_e.at[lt - 1, band], e_fl.at[band], rt),
        )
        for c in e_copies[q]:
            c.start()

    for s in range(3):
        for t in range(lt):
            ion_copy(s, t).wait()

    @pl.when(has_up)
    def _():
        i_up.start()

    @pl.when(has_dn)
    def _():
        i_dn.start()

    i_lf.start()
    i_rt.start()

    @pl.when(jnp.logical_not(has_up))
    def _():
        cur_n[:, 0:8, :] = jnp.zeros((lt, 8, 128), F32)
        ion[:, :, 0:8, :] = jnp.zeros((3, lt, 8, 128), F32)
        S[:, 0:GUARD, :] = jnp.zeros((nt, GUARD, 128), F32)
        src[:, 0:GUARD, :] = jnp.zeros((nt, GUARD, 128), F32)

    @pl.when(jnp.logical_not(has_dn))
    def _():
        cur_n[:, rows + 8 : rows + 16, :] = jnp.zeros((lt, 8, 128), F32)
        ion[:, :, rows + 8 : rows + 16, :] = jnp.zeros((3, lt, 8, 128), F32)
        S[:, GUARD + rows :, :] = jnp.zeros((nt, GUARD, 128), F32)
        src[:, GUARD + rows :, :] = jnp.zeros((nt, GUARD, 128), F32)

    @pl.when(has_dn)
    def _():
        n_up.wait_recv()

    @pl.when(has_up)
    def _():
        n_dn.wait_recv()

    t_copies = {}
    for q in piece_order:
        for c in e_copies[q]:
            c.wait_recv()

        @pl.loop(q * per, (q + 1) * per, unroll=per)
        def _(c):
            row = pl.multiple_of(8 * c, 8)
            at = pl.ds(row, 8)
            tiles = [cur_e[t, at, :] for t in range(lt)]
            tiles.append(jnp.where(lane < 64, e_fr[at, :], e_fl[at, :]))
            left, right = shifts(tiles)
            for t in range(lt):
                d_lon = 0.5 * (right[t] - left[t])
                d_lat = 0.5 * (cur_n[t, pl.ds(row + 9, 8), :] - cur_n[t, pl.ds(row + 7, 8), :])
                s_one[t, at, :] = d_lon + d_lat
                t_out[t, at, :] = d_lon - d_lat

        band = slice(q * per * 8, (q + 1) * per * 8)
        t_copies[q] = rcopy(t_out.at[:, band], t_rx.at[:, band], mirror)
        t_copies[q].start()

    for j in range(nt):
        @pl.loop(0, 8, unroll=2)
        def _(c):
            row = lax.broadcasted_iota(jnp.int32, (16, 128), 0) + 16 * c
            col = lax.broadcasted_iota(jnp.int32, (16, 128), 1)
            home = row * nt + j
            for t in range(lt):
                here = col + t * 128
                back = jnp.where(home == here, 1.0, 0.0).astype(BF16)
                before = jnp.where(here == 0, width - 1, here - 1)
                slope = jnp.where(
                    home == here + 1, 0.5, jnp.where(home == before, -0.5, 0.0)
                ).astype(BF16)
                for part in range(3):
                    at = pl.ds(pl.multiple_of(part * width + j * 128 + 16 * c, 16), 16)
                    to_plain[at, t * 128 : (t + 1) * 128] = back
                    to_plain[at, (lt + t) * 128 : (lt + t + 1) * 128] = slope

    i_lf.wait_recv()
    i_rt.wait_recv()
    for s in range(3):
        @pl.loop(0, n_rt, unroll=4)
        def _(c):
            row = pl.multiple_of(8 * c, 8)
            at = pl.ds(row, 8)
            tiles = [ion[s, t, pl.ds(row + 8, 8), :] for t in range(lt)]
            tiles.append(jnp.where(lane < 64, ion_fr[s, at, :], ion_fl[s, at, :]))
            left, right = shifts(tiles)
            for t in range(lt):
                ion_a[s, t, at, :] = tiles[t] - left[t]
                ion_b[s, t, at, :] = right[t] - tiles[t]

    def combine(own, rx, out, q):
        @pl.loop((PIECES - 1 - q) * per, (PIECES - q) * per, unroll=per)
        def _(c):
            row = pl.multiple_of(8 * c, 8)
            back = pl.multiple_of(rows - 8 - 8 * c, 8)
            for t in range(lt):
                out[t, pl.ds(row + GUARD, 8), :] = own[t, pl.ds(row, 8), :] + rev8(
                    rx[t, pl.ds(back, 8), :]
                )

    def exchange(own, rx, copies, out, fr, fl, depth):
        lo_in, hi_in = slice(GUARD, GUARD + depth), slice(GUARD + rows - depth, GUARD + rows)
        lo_out, hi_out = slice(GUARD - depth, GUARD), slice(GUARD + rows, GUARD + rows + depth)
        c_up = rcopy(out.at[0:lt, lo_in], out.at[0:lt, hi_out], up)
        c_dn = rcopy(out.at[0:lt, hi_in], out.at[0:lt, lo_out], dn)
        lons = []

        def send_lon(part):
            lons.append(rcopy(out.at[0, part], fr.at[part], lf))
            lons.append(rcopy(out.at[lt - 1, part], fl.at[part], rt))
            lons[-2].start()
            lons[-1].start()

        def first(i):
            q = piece_order[i]
            copies[q].wait_recv()
            combine(own, rx, out, q)
            lo = GUARD + (PIECES - 1 - q) * per * 8
            if q == PIECES - 1:
                @pl.when(has_up)
                def _():
                    c_up.start()
            if q == 0:
                @pl.when(has_dn)
                def _():
                    c_dn.start()
            send_lon(slice(lo, lo + per * 8))

        def edges():
            @pl.when(has_up)
            def _():
                c_dn.wait_recv()

            send_lon(lo_out)

            @pl.when(has_dn)
            def _():
                c_up.wait_recv()

            send_lon(hi_out)

        first(0)
        first(1)
        for i in range(2, PIECES):
            first(i)
            if i == 2:
                edges()
        for c in lons:
            c.wait_recv()

        @pl.loop((GUARD - depth) // 8, (GUARD + rows + depth) // 8, unroll=4)
        def _(c):
            at = pl.ds(pl.multiple_of(8 * c, 8), 8)
            out[lt, at, :] = jnp.where(lane < 64, fr[at, :], fl[at, :])

        return c_up, c_dn, lons

    def split(v, at, t):
        for part in range(3):
            low = v.astype(BF16)
            lhs[at, part * width + t * 128 : part * width + (t + 1) * 128] = low
            v = v - low.astype(F32)

    def split_rows(ref, first, count):
        @pl.loop(0, count // 16, unroll=2)
        def _(c):
            row = pl.multiple_of(16 * c, 16)
            for t in range(nt):
                split(ref[t, pl.ds(pl.multiple_of(row + first, 8), 16), :], pl.ds(row, 16), t)

    def conv_lon(v):
        after = v[1:] + [pltpu.roll(v[0], 127, 1)]
        p = [a + b for a, b in zip(v, after)]
        before = [pltpu.roll(p[-1], 1, 1)] + p[:-1]
        return [a + b for a, b in zip(p, before)]

    s_up, s_dn, s_lons = exchange(sig, sig_rx, sig_copies, S, s_fr, s_fl, GUARD)
    tall = rows + 2 * GUARD
    ext = rows + 2 * HALO
    split_rows(S, 0, tall)
    moved = jnp.dot(lhs[0:tall, :], to_strided[...], preferred_element_type=F32)
    for t in range(nt):
        SP[t, :, :] = moved[:, t * 128 : (t + 1) * 128]

    @pl.loop(0, tall // 8, unroll=2)
    def _(c):
        at = pl.ds(pl.multiple_of(8 * c, 8), 8)
        for t, v in enumerate(conv_lon([SP[t, at, :] for t in range(nt)])):
            U[t, at, :] = v

    total = rows * nlat
    skip = GUARD - HALO
    for c in range(R):
        where = sub * R + (c - HALO + me_lat * rows)
        inside = (where >= 0) & (where < total)
        at = slice(8 * c, 8 * c + 8)
        for t in range(nt):
            s = SP[t, pl.ds(skip + c, 8, stride=R), :]
            around = U[t, pl.ds(skip + c - 1, 8, stride=R), :] + U[
                t, pl.ds(skip + c + 1, 8, stride=R), :
            ]
            around = around + 2.0 * U[t, pl.ds(skip + c, 8, stride=R), :]
            inv = jnp.where(inside, 1.0 / (DAMPING + 2.0 * s + 0.25 * around), 0.0)
            quarter = 0.25 * inv
            SR[t, at, :] = s
            invR[t, at, :] = inv
            rR[t, at, :] = quarter
            mR[t, at, :] = (THETA - 1.0) - 8.0 * (quarter * s)
            X[1, t, at, :] = jnp.zeros((8, 128), F32)

    v_up, v_dn, v_lons = exchange(s_one, t_rx, t_copies, src, v_fr, v_fl, HALO)
    split_rows(src, skip, ext)
    moved = jnp.dot(lhs[0:ext, :], to_strided[...], preferred_element_type=F32)
    for t in range(nt):
        SP[t, 0:ext, :] = moved[:, t * 128 : (t + 1) * 128]
    for c in range(R):
        at = slice(8 * c, 8 * c + 8)
        for t in range(nt):
            first = SP[t, pl.ds(c, 8, stride=R), :] * invR[t, at, :]
            spR[t, at, :] = first
            X[0, t, at, :] = first * (1.0 / THETA)

    def sweep(k, cur, prv, final):
        c1 = coef[0, k]
        c2 = coef[1, k]

        def smooth(c):
            at = slice(8 * c, 8 * c + 8)
            xs = [X[cur, t, at, :] for t in range(nt)]
            ys = [SR[t, at, :] * xs[t] for t in range(nt)]
            return xs, conv_lon(xs), conv_lon(ys)

        _, u_end, w_end = smooth(R - 1)
        xs, u, w = smooth(0)
        u_top, w_top = u, w
        qu = [pltpu.roll(a, 1, 0) + b for a, b in zip(u_end, u)]
        qw = [pltpu.roll(a, 1, 0) + b for a, b in zip(w_end, w)]
        for c in range(R):
            if c < R - 1:
                x_next, u_next, w_next = smooth(c + 1)
            else:
                x_next = None
                u_next = [pltpu.roll(v, 7, 0) for v in u_top]
                w_next = [pltpu.roll(v, 7, 0) for v in w_top]
            qu2 = [a + b for a, b in zip(u, u_next)]
            qw2 = [a + b for a, b in zip(w, w_next)]
            at = slice(8 * c, 8 * c + 8)
            for t in range(nt):
                pull = SR[t, at, :] * (qu[t] + qu2[t]) + (qw[t] + qw2[t])
                z = rR[t, at, :] * pull + (mR[t, at, :] * xs[t] + spR[t, at, :])
                new = c2 * z - c1 * X[prv, t, at, :]
                if final:
                    xr[t, pl.ds(8 + c, 8, stride=R), :] = new
                else:
                    X[prv, t, at, :] = new
            qu, qw, u, w, xs = qu2, qw2, u_next, w_next, x_next

    @pl.loop(0, (SWEEPS - 2) // 2)
    def _(k):
        sweep(2 * k, 0, 1, False)
        sweep(2 * k + 1, 1, 0, False)

    sweep(SWEEPS - 2, 0, 1, True)

    own0 = 8 + HALO
    best = jnp.zeros((8, 128), F32)
    for c in range(n_rt):
        lo = own0 + 8 * c
        x = [xr[t, lo : lo + 8, :] for t in range(nt)]
        after = x[1:] + [pltpu.roll(x[0], 127, 1)]
        before = [pltpu.roll(x[-1], 1, 1)] + x[:-1]
        for t in range(nt):
            speed = jnp.abs(0.5 * (xr[t, lo + 1 : lo + 9, :] - xr[t, lo - 1 : lo + 7, :]))
            speed = speed + jnp.abs(0.5 * (after[t] - before[t]))
            best = jnp.maximum(best, jnp.where(lane * nt + t < lt * 128, speed, 0.0))
    mx[0:1, :] = jnp.max(best, axis=0, keepdims=True)

    max_copies = []
    for o, dev in enumerate(others):
        max_copies.append(
            pltpu.make_async_remote_copy(
                src_ref=mx.at[0:1], dst_ref=mrx.at[o : o + 1],
                send_sem=ss_max.at[o], recv_sem=rs_max.at[o],
                device_id=dev, device_id_type=MESH,
            )
        )
        max_copies[-1].start()

    near = rows + 16
    split_rows(xr, own0 - 8, near)
    moved = jnp.dot(lhs[0:near, :], to_plain[...], preferred_element_type=F32)
    for t in range(lt):
        xn[t, :, :] = moved[:, t * 128 : (t + 1) * 128]
        dnb[t, :, :] = moved[:, (lt + t) * 128 : (lt + t + 1) * 128]
        pot_o[:, t * 128 : (t + 1) * 128] = moved[8 : 8 + rows, t * 128 : (t + 1) * 128]

    @pl.when(has_dn)
    def _():
        i_up.wait_recv()

    @pl.when(has_up)
    def _():
        i_dn.wait_recv()

    @pl.loop(0, n_rt, unroll=2)
    def _(c):
        row = pl.multiple_of(8 * c, 8)
        at = pl.ds(row, 8)
        for t in range(lt):
            de = -0.5 * (xn[t, pl.ds(row + 9, 8), :] - xn[t, pl.ds(row + 7, 8), :])
            dv = dnb[t, pl.ds(row + 8, 8), :]
            e_pos, e_neg = jnp.maximum(de, 0.0), jnp.minimum(de, 0.0)
            n_pos, n_neg = jnp.maximum(dv, 0.0), jnp.minimum(dv, 0.0)
            for s in range(3):
                n = ion[s, t, pl.ds(row + 8, 8), :]
                f = e_pos * ion_a[s, t, at, :] + e_neg * ion_b[s, t, at, :]
                f = f + n_pos * (n - ion[s, t, pl.ds(row + 7, 8), :])
                f = f + n_neg * (ion[s, t, pl.ds(row + 9, 8), :] - n)
                flux[s, t, at, :] = f

    for c in max_copies:
        c.wait_recv()
    best = jnp.maximum(
        jnp.max(mrx[0 : n_dev - 1, :], axis=0, keepdims=True), mx[0:1, :]
    )
    best = jnp.max(best, axis=1, keepdims=True)
    step = jnp.broadcast_to(COURANT / (best + 1e-6), (8, 128))

    for s in range(3):
        scale = MOBILITY[s] * step

        @pl.loop(0, n_rt, unroll=2)
        def _(c):
            row = pl.multiple_of(8 * c, 8)
            for t in range(lt):
                upd_o[s, pl.ds(row, 8), t * 128 : (t + 1) * 128] = (
                    ion[s, t, pl.ds(row + 8, 8), :] - scale * flux[s, t, pl.ds(row, 8), :]
                )

    @pl.when(has_up)
    def _():
        for c in (n_up, i_up, s_up, v_up):
            c.wait_send()

    @pl.when(has_dn)
    def _():
        for c in (n_dn, i_dn, s_dn, v_dn):
            c.wait_send()

    done = [i_lf, i_rt] + s_lons + v_lons + max_copies
    for q in piece_order:
        done += [sig_copies[q], t_copies[q]] + list(e_copies[q])
    for c in done:
        c.wait_send()


def solution(mesh):
    nlat, nlon = mesh.shape["lat"], mesh.shape["lon"]

    def shards(pedersen, hall_conductivity, east_wind, north_wind, ion_density):
        lev, rows, cols = pedersen.shape
        lt = cols // 128
        nt = lt + 1
        width = nt * 128
        tall = rows + 2 * GUARD
        ext = rows + 2 * HALO
        others = nlat * nlon - 1
        vm = lambda *shape: pltpu.VMEM(shape, F32)
        half = lambda *shape: pltpu.VMEM(shape, BF16)
        dma = lambda *shape: pltpu.SemaphoreType.DMA(shape)
        hbm = pl.BlockSpec(memory_space=pltpu.HBM)
        return pl.pallas_call(
            functools.partial(kernel, nlat, nlon, lev, rows, lt),
            out_shape=(pltpu.VMEM((rows, cols), F32), pltpu.VMEM((3, rows, cols), F32)),
            in_specs=[hbm] * 5,
            out_specs=(pl.BlockSpec(memory_space=pltpu.VMEM),) * 2,
            scratch_shapes=[vm(lev, rows, cols)] * 4
            + [vm(3, lt, rows + 16, 128)] + [vm(3, rows, 128)] * 2 + [vm(3, lt, rows, 128)] * 2
            + [vm(lt, rows, 128), vm(lt, rows, 128), vm(lt, rows + 16, 128)]
            + [vm(rows, 128)] * 2
            + [vm(lt, rows, 128)] * 4
            + [vm(nt, tall, 128)] * 2 + [vm(tall, 128)] * 4
            + [half(tall, 3 * width), half(3 * width, width), half(3 * width, 2 * lt * 128)]
            + [pltpu.SMEM((2, SWEEPS), F32)]
            + [vm(nt, tall, 128)] * 2
            + [vm(nt, ext, 128)] * 5
            + [vm(2, nt, ext, 128), vm(nt, ext + 16, 128)]
            + [vm(lt, rows + 16, 128)] * 2
            + [vm(3, lt, rows, 128), vm(8, 128), vm(others + 1, 128)]
            + [dma(rows // 8, 4), dma(3, lt), dma(54), dma(54), dma(others), dma(others)],
            compiler_params=pltpu.CompilerParams(
                collective_id=0, has_side_effects=True, vmem_limit_bytes=60 * 1024 * 1024
            ),
        )(pedersen, hall_conductivity, east_wind, north_wind, ion_density)

    spec = P(None, "lat", "lon")
    return jax.shard_map(
        shards,
        mesh=mesh,
        in_specs=(spec,) * 5,
        out_specs=(P("lat", "lon"), spec),
        check_vma=False,
    )
```

```python
import functools

import jax
import jax.numpy as jnp
from jax import lax
from jax.experimental import pallas as pl
from jax.experimental.pallas import tpu as pltpu
from jax.sharding import PartitionSpec as P

SWEEPS = 16
DAMPING = 0.0001
LOW_BOUND = 0.05
HIGH_BOUND = 2.0
COURANT = 0.8
MOBILITY = (1.0, 0.6, 0.3)
MESH = pl.DeviceIdType.MESH
GUARD = 24
HALO = 16
PIECES = 4
THETA = 0.5 * (HIGH_BOUND + LOW_BOUND)
F32 = jnp.float32
BF16 = jnp.bfloat16


def chebyshev_factors():
    delta = 0.5 * (HIGH_BOUND - LOW_BOUND)
    sigma_one = THETA / delta
    rho_prev = 1.0 / sigma_one
    first_list = []
    second_list = []
    for sweep in range(SWEEPS):
        rho_next = 1.0 / (2.0 * sigma_one - rho_prev)
        first_list.append(rho_next * rho_prev)
        second_list.append(2.0 * rho_next / delta)
        rho_prev = rho_next
    return first_list, second_list


RECV = ("e", "ion", "n_up", "n_dn", "i_up", "i_dn", "sig_a", "sig_b", "t_a", "t_b", "t_c",
        "s_up", "s_dn", "s_lon", "v_up", "v_dn", "v_lon", "v_last", "max")
SEND = ("sig", "t", "lon", "up", "dn", "max")
EDGE = 32


def in_groups(n_rt):
    per = n_rt // PIECES
    spans = [(0, 1), (n_rt - 1, n_rt), (1, per), (n_rt - per, n_rt - 1)]
    for q in range(1, PIECES - 1):
        half = q * per + per // 2
        spans += [(q * per, half), (half, (q + 1) * per)]
    return [p for p in spans if p[1] > p[0]]


def kernel(
    nlat, nlon, lev, rows, lt,
    ped_h, hall_h, east_h, north_h, ion_h,
    pot_o, upd_o,
    vin, ion, ion_a, ion_b,
    sig, cur_e, cur_n, s_one, t_out, sig_rx, t_rx,
    S, src, pk, rx_e, rx_ion, rx_s, rx_v,
    lhs, to_strided, to_plain, coef,
    SP, U, SR, rR, mR, invR, spR, X, xr, xn, dnb,
    flux, mx, mrx,
    sem_in, sem_ion, ss, rs,
):
    n_rt = rows // 8
    nt = lt + 1
    width = nt * 128
    R = (rows + 2 * HALO) // 8
    n_dev = nlat * nlon
    me_lat = lax.axis_index("lat")
    me_lon = lax.axis_index("lon")
    has_up = me_lat > 0
    has_dn = me_lat < nlat - 1
    up = (jnp.maximum(me_lat - 1, 0), me_lon)
    dn = (jnp.minimum(me_lat + 1, nlat - 1), me_lon)
    lf = (me_lat, lax.rem(me_lon + nlon - 1, nlon))
    rt = (me_lat, lax.rem(me_lon + 1, nlon))
    mirror = (nlat - 1 - me_lat, me_lon)
    others = [
        (lax.rem(me_lat + a, nlat), lax.rem(me_lon + b, nlon))
        for a in range(nlat) for b in range(nlon) if a or b
    ]

    barrier = pltpu.get_barrier_semaphore()
    for dev in others:
        pl.semaphore_signal(barrier, inc=1, device_id=dev, device_id_type=MESH)

    per = n_rt // PIECES
    groups = in_groups(n_rt)

    def in_copy(a, g):
        at = slice(8 * groups[g][0], 8 * groups[g][1])
        return pltpu.make_async_copy(
            (ped_h, hall_h, east_h, north_h)[a].at[:, at, :], vin.at[a, :, at, :], sem_in.at[g]
        )

    for g in range(len(groups)):
        for a in range(4):
            in_copy(a, g).start()
    for s in range(3):
        for t in range(lt):
            pltpu.make_async_copy(
                ion_h.at[s, :, t * 128 : (t + 1) * 128], ion.at[s, t, 8 : 8 + rows], sem_ion.at[0]
            ).start()

    first_list, second_list = chebyshev_factors()
    for k in range(SWEEPS):
        coef[0, k] = jnp.float32(first_list[k])
        coef[1, k] = jnp.float32(second_list[k])

    def rcopy(src_ref, dst_ref, dev, send, recv):
        return pltpu.make_async_remote_copy(
            src_ref=src_ref, dst_ref=dst_ref,
            send_sem=ss.at[SEND.index(send)], recv_sem=rs.at[RECV.index(recv)],
            device_id=dev, device_id_type=MESH,
        )

    def arrived(name, view):
        pltpu.make_async_copy(view, view, rs.at[RECV.index(name)]).wait()

    def sent(name, view):
        pltpu.make_async_copy(view, view, ss.at[SEND.index(name)]).wait()

    lane = lax.broadcasted_iota(jnp.int32, (8, 128), 1)
    sub = lax.broadcasted_iota(jnp.int32, (8, 128), 0)

    def turn(v, by):
        by = by % 128
        return pltpu.roll(v, by, 1) if by else v

    def shifts(v, after, before):
        a = [pltpu.roll(t, 1, 1) for t in v]
        b = [pltpu.roll(t, 127, 1) for t in v] + [after]
        left = [jnp.where(lane == 0, p, q) for p, q in zip([before] + a[:-1], a)]
        right = [jnp.where(lane == 127, p, q) for p, q in zip(b[1:], b[:-1])]
        return left, right

    def pack(slot, tiles, step, skip):
        acc = None
        for k, v in enumerate(tiles):
            v = turn(v, step * k + skip)
            acc = v if k == 0 else jnp.where(lane < step * k, acc, v)
        pk[slot, :, :] = acc

    def rev8(v):
        v = pltpu.roll(v, 4, 0)
        for b in (2, 1):
            v = jnp.where((sub & b) == 0, pltpu.roll(v, 8 - b, 0), pltpu.roll(v, b, 0))
        return v

    @pl.loop(0, width // 16, unroll=4)
    def _(c):
        row = lax.broadcasted_iota(jnp.int32, (16, 128), 0) + 16 * c
        col = lax.broadcasted_iota(jnp.int32, (16, 128), 1)
        for t in range(nt):
            there = jnp.where(row == col * nt + t, 1.0, 0.0).astype(BF16)
            for part in range(3):
                at = pl.ds(pl.multiple_of(part * width + 16 * c, 16), 16)
                to_strided[at, t * 128 : (t + 1) * 128] = there

    weight = [(0.5 + l / lev) / lev for l in range(lev)]

    def columns(g):
        lo, hi = groups[g]
        view = vin.at[:, :, 8 * lo : 8 * hi, :]
        pltpu.make_async_copy(view, view, sem_in.at[g]).wait()

        @pl.loop(lo, hi)
        def _(c):
            row = pl.multiple_of(8 * c, 8)
            for t in range(lt):
                at = (pl.ds(row, 8), slice(t * 128, (t + 1) * 128))
                acc = [jnp.zeros((8, 128), F32)] * 3
                for l in range(lev):
                    p, h = weight[l] * vin[(0, l) + at], weight[l] * vin[(1, l) + at]
                    e, n = vin[(2, l) + at], vin[(3, l) + at]
                    acc = [acc[0] + p, acc[1] + (p * e + h * n), acc[2] + (p * n - h * e)]
                sig[t, pl.ds(row, 8), :] = acc[0]
                cur_e[t, pl.ds(row, 8), :] = acc[1]
                cur_n[t, pl.ds(row + 8, 8), :] = acc[2]

    def band(q):
        return slice(q * per * 8, (q + 1) * per * 8)

    def send_sig(q, recv):
        rcopy(sig.at[:, band(q)], sig_rx.at[:, band(q)], mirror, "sig", recv).start()

    def send_t(q, recv):
        rcopy(t_out.at[:, band(q)], t_rx.at[:, band(q)], mirror, "t", recv).start()

    def to_up(src_ref, dst_ref, recv):
        @pl.when(has_up)
        def _():
            rcopy(src_ref, dst_ref, up, "up", recv).start()

    def to_dn(src_ref, dst_ref, recv):
        @pl.when(has_dn)
        def _():
            rcopy(src_ref, dst_ref, dn, "dn", recv).start()

    def from_dn(name, view):
        @pl.when(has_dn)
        def _():
            arrived(name, view)

    def from_up(name, view):
        @pl.when(has_up)
        def _():
            arrived(name, view)

    def send_lon(slot, rx, g, recv):
        rcopy(pk.at[slot], rx.at[0, g], lf, "lon", recv).start()
        rcopy(pk.at[slot + 1], rx.at[1, g], rt, "lon", recv).start()

    columns(0)
    columns(1)
    pl.semaphore_wait(barrier, n_dev - 1)
    to_up(cur_n.at[:, 8:16], cur_n.at[:, rows + 8 : rows + 16], "n_up")
    to_dn(cur_n.at[:, rows : rows + 8], cur_n.at[:, 0:8], "n_dn")
    columns(2)
    send_sig(0, "sig_a")
    columns(3)
    send_sig(PIECES - 1, "sig_a")
    for q in range(1, PIECES - 1):
        columns(2 * q + 2)
        columns(2 * q + 3)
        send_sig(q, "sig_b")

    step_e = 128 // n_rt
    pack(0, [cur_e[0, 8 * c : 8 * c + 8, :] for c in range(n_rt)], step_e, 0)
    pack(1, [cur_e[lt - 1, 8 * c : 8 * c + 8, :] for c in range(n_rt)], step_e, 1)
    send_lon(0, rx_e, 0, "e")

    @pl.when(jnp.logical_not(has_up))
    def _():
        cur_n[:, 0:8, :] = jnp.zeros((lt, 8, 128), F32)
        ion[:, :, 0:8, :] = jnp.zeros((3, lt, 8, 128), F32)
        S[:, 0:GUARD, :] = jnp.zeros((nt, GUARD, 128), F32)
        src[:, 0:GUARD, :] = jnp.zeros((nt, GUARD, 128), F32)

    @pl.when(jnp.logical_not(has_dn))
    def _():
        cur_n[:, rows + 8 : rows + 16, :] = jnp.zeros((lt, 8, 128), F32)
        ion[:, :, rows + 8 : rows + 16, :] = jnp.zeros((3, lt, 8, 128), F32)
        S[:, GUARD + rows :, :] = jnp.zeros((nt, GUARD, 128), F32)
        src[:, GUARD + rows :, :] = jnp.zeros((nt, GUARD, 128), F32)

    view = ion.at[:, :, 8 : 8 + rows]
    pltpu.make_async_copy(view, view, sem_ion.at[0]).wait()
    step_i = 128 // (3 * n_rt)
    bands = [(s, c) for s in range(3) for c in range(n_rt)]
    pack(2, [ion[s, 0, 8 * c + 8 : 8 * c + 16, :] for s, c in bands], step_i, 0)
    pack(3, [ion[s, lt - 1, 8 * c + 8 : 8 * c + 16, :] for s, c in bands], step_i, 1)
    send_lon(2, rx_ion, 0, "ion")

    from_dn("n_up", cur_n.at[:, 0:8])
    from_up("n_dn", cur_n.at[:, 0:8])
    arrived("e", rx_e)
    e_fr, e_fl = rx_e[0, 0, :, :], rx_e[1, 0, :, :]
    for q in [0, PIECES - 1] + list(range(1, PIECES - 1)):
        for c in range(q * per, (q + 1) * per):
            row = 8 * c
            at = slice(row, row + 8)
            left, right = shifts(
                [cur_e[t, at, :] for t in range(lt)],
                turn(e_fr, 127 - step_e * c), turn(e_fl, 128 - step_e * c),
            )
            for t in range(lt):
                d_lon = 0.5 * (right[t] - left[t])
                d_lat = 0.5 * (cur_n[t, row + 9 : row + 17, :] - cur_n[t, row + 7 : row + 15, :])
                s_one[t, at, :] = d_lon + d_lat
                t_out[t, at, :] = d_lon - d_lat
        if q in (0, PIECES - 1):
            send_t(q, "t_a")

    for j in range(nt):
        @pl.loop(0, 8, unroll=2)
        def _(c):
            row = lax.broadcasted_iota(jnp.int32, (16, 128), 0) + 16 * c
            col = lax.broadcasted_iota(jnp.int32, (16, 128), 1)
            home = row * nt + j
            for t in range(lt):
                here = col + t * 128
                back = jnp.where(home == here, 1.0, 0.0).astype(BF16)
                before = jnp.where(here == 0, width - 1, here - 1)
                slope = jnp.where(
                    home == here + 1, 0.5, jnp.where(home == before, -0.5, 0.0)
                ).astype(BF16)
                for part in range(3):
                    at = pl.ds(pl.multiple_of(part * width + j * 128 + 16 * c, 16), 16)
                    to_plain[at, t * 128 : (t + 1) * 128] = back
                    to_plain[at, (lt + t) * 128 : (lt + t + 1) * 128] = slope

    def combine(own, rx, out, q):
        p = PIECES - 1 - q
        for c in range(p * per, (p + 1) * per):
            back = rows - 8 - 8 * c
            for t in range(lt):
                out[t, 8 * c + GUARD : 8 * c + GUARD + 8, :] = own[
                    t, 8 * c : 8 * c + 8, :
                ] + rev8(rx[t, back : back + 8, :])

    def spread(out, rx, slot, g, lo, count, recv):
        tiles = lambda t: [out[t, lo + 8 * k : lo + 8 * k + 8, :] for k in range(count)]
        pack(slot, tiles(0), EDGE, 0)
        pack(slot + 1, tiles(lt - 1), EDGE, EDGE)
        send_lon(slot, rx, g, recv)

    def gather(out, rx, g, lo, count):
        fr, fl = rx[0, g, :, :], rx[1, g, :, :]
        for k in range(count):
            a, b = turn(fr, 128 - EDGE * k), turn(fl, 256 - EDGE - EDGE * k)
            out[lt, lo + 8 * k : lo + 8 * k + 8, :] = jnp.where(
                lane < EDGE, a, jnp.where(lane >= 128 - EDGE, b, 0.0)
            )

    def spread_piece(out, rx, slot, q, recv):
        p = PIECES - 1 - q
        spread(out, rx, slot + 2 * p, p, GUARD + p * per * 8, per, recv)

    def gather_piece(out, rx, q):
        p = PIECES - 1 - q
        gather(out, rx, p, GUARD + p * per * 8, per)

    def lat_send(out, depth, name):
        lo, hi = GUARD, GUARD + rows
        to_up(out.at[0:lt, lo : lo + depth], out.at[0:lt, hi : hi + depth], name + "_up")
        to_dn(out.at[0:lt, hi - depth : hi], out.at[0:lt, lo - depth : lo], name + "_dn")

    def lat_spread(out, rx, depth, name, slot):
        lo, hi = GUARD, GUARD + rows
        from_up(name + "_dn", out.at[0:lt, lo - depth : lo])
        spread(out, rx, slot + 2 * PIECES, PIECES, lo - depth, depth // 8, name + "_lon")
        from_dn(name + "_up", out.at[0:lt, lo - depth : lo])
        spread(out, rx, slot + 2 * PIECES + 2, PIECES + 1, hi, depth // 8, name + "_lon")

    def lat_gather(out, rx, depth):
        gather(out, rx, PIECES, GUARD - depth, depth // 8)
        gather(out, rx, PIECES + 1, GUARD + rows, depth // 8)

    outer, inner = [0, PIECES - 1], list(range(1, PIECES - 1))
    slot_s, slot_v = 4, 4 + 2 * (PIECES + 2)

    arrived("sig_a", sig_rx.at[:, 0 : 2 * per * 8])
    for q in outer:
        combine(sig, sig_rx, S, q)
    lat_send(S, GUARD, "s")
    for q in inner[:-1]:
        send_t(q, "t_b")
    for q in outer:
        spread_piece(S, rx_s, slot_s, q, "s_lon")
    arrived("sig_b", sig_rx.at[:, 0 : (PIECES - 2) * per * 8])
    for q in inner:
        combine(sig, sig_rx, S, q)
        spread_piece(S, rx_s, slot_s, q, "s_lon")

    arrived("ion", rx_ion)
    i_fr, i_fl = rx_ion[0, 0, :, :], rx_ion[1, 0, :, :]
    for k, (s, c) in enumerate(bands):
        at = slice(8 * c, 8 * c + 8)
        tiles = [ion[s, t, 8 * c + 8 : 8 * c + 16, :] for t in range(lt)]
        left, right = shifts(tiles, turn(i_fr, 127 - step_i * k), turn(i_fl, 128 - step_i * k))
        for t in range(lt):
            ion_a[s, t, at, :] = tiles[t] - left[t]
            ion_b[s, t, at, :] = right[t] - tiles[t]

    lat_spread(S, rx_s, GUARD, "s", slot_s)
    arrived("s_lon", rx_s)
    for q in outer + inner:
        gather_piece(S, rx_s, q)
    lat_gather(S, rx_s, GUARD)

    def split(v, at, t):
        for part in range(3):
            low = v.astype(BF16)
            lhs[at, part * width + t * 128 : part * width + (t + 1) * 128] = low
            v = v - low.astype(F32)

    def split_rows(ref, first, lo, hi):
        for row in range(lo, hi, 16):
            for t in range(nt):
                split(ref[t, row + first : row + first + 16, :], slice(row, row + 16), t)

    def conv_lon(v):
        after = v[1:] + [pltpu.roll(v[0], 127, 1)]
        p = [a + b for a, b in zip(v, after)]
        before = [pltpu.roll(p[-1], 1, 1)] + p[:-1]
        return [a + b for a, b in zip(p, before)]

    tall = rows + 2 * GUARD
    ext = rows + 2 * HALO
    split_rows(S, 0, 0, tall)
    moved = jnp.dot(lhs[0:tall, :], to_strided[...], preferred_element_type=F32)
    for t in range(nt):
        SP[t, :, :] = moved[:, t * 128 : (t + 1) * 128]

    for c in range(tall // 8):
        for t, v in enumerate(conv_lon([SP[t, 8 * c : 8 * c + 8, :] for t in range(nt)])):
            U[t, 8 * c : 8 * c + 8, :] = v

    total = rows * nlat
    skip = GUARD - HALO
    for c in range(R):
        where = sub * R + (c - HALO + me_lat * rows)
        inside = (where >= 0) & (where < total)
        at = slice(8 * c, 8 * c + 8)
        for t in range(nt):
            s = SP[t, pl.ds(skip + c, 8, stride=R), :]
            around = U[t, pl.ds(skip + c - 1, 8, stride=R), :] + U[
                t, pl.ds(skip + c + 1, 8, stride=R), :
            ]
            around = around + 2.0 * U[t, pl.ds(skip + c, 8, stride=R), :]
            inv = jnp.where(inside, 1.0 / (DAMPING + 2.0 * s + 0.25 * around), 0.0)
            quarter = 0.25 * inv
            SR[t, at, :] = s
            invR[t, at, :] = inv
            rR[t, at, :] = quarter
            mR[t, at, :] = (THETA - 1.0) - 8.0 * (quarter * s)
            X[1, t, at, :] = jnp.zeros((8, 128), F32)

    arrived("t_a", t_rx.at[:, 0 : 2 * per * 8])
    for q in outer:
        combine(s_one, t_rx, src, q)
    lat_send(src, HALO, "v")
    send_t(inner[-1], "t_c")
    to_up(ion.at[:, :, 8:16], ion.at[:, :, rows + 8 : rows + 16], "i_up")
    to_dn(ion.at[:, :, rows : rows + 8], ion.at[:, :, 0:8], "i_dn")
    for q in outer:
        spread_piece(src, rx_v, slot_v, q, "v_lon")
    arrived("t_b", t_rx.at[:, 0 : (PIECES - 3) * per * 8])
    for q in inner[:-1]:
        combine(s_one, t_rx, src, q)
        spread_piece(src, rx_v, slot_v, q, "v_lon")
    lat_spread(src, rx_v, HALO, "v", slot_v)
    arrived("v_lon", pk.at[0 : 2 * (PIECES + 1)])
    for q in outer + inner[:-1]:
        gather_piece(src, rx_v, q)
    lat_gather(src, rx_v, HALO)
    last = PIECES - 1 - inner[-1]
    last_lo, last_hi = HALO + last * per * 8, HALO + (last + 1) * per * 8
    for lo, hi in ((0, last_lo), (last_hi, ext)):
        split_rows(src, skip, lo, hi)
        moved = jnp.dot(lhs[lo:hi, :], to_strided[...], preferred_element_type=F32)
        for t in range(nt):
            SP[t, lo:hi, :] = moved[:, t * 128 : (t + 1) * 128]

    arrived("t_c", t_rx.at[:, 0 : per * 8])
    combine(s_one, t_rx, src, inner[-1])
    spread_piece(src, rx_v, slot_v, inner[-1], "v_last")
    arrived("v_last", pk.at[0:2])
    gather_piece(src, rx_v, inner[-1])
    split_rows(src, skip, last_lo, last_hi)
    moved = jnp.dot(lhs[last_lo:last_hi, :], to_strided[...], preferred_element_type=F32)
    for t in range(nt):
        SP[t, last_lo:last_hi, :] = moved[:, t * 128 : (t + 1) * 128]
    for c in range(R):
        at = slice(8 * c, 8 * c + 8)
        for t in range(nt):
            first = SP[t, pl.ds(c, 8, stride=R), :] * invR[t, at, :]
            spR[t, at, :] = first
            X[0, t, at, :] = first * (1.0 / THETA)

    def sweep(k, cur, prv, final):
        c1 = coef[0, k]
        c2 = coef[1, k]

        def smooth(c):
            at = slice(8 * c, 8 * c + 8)
            xs = [X[cur, t, at, :] for t in range(nt)]
            ys = [SR[t, at, :] * xs[t] for t in range(nt)]
            return xs, conv_lon(xs), conv_lon(ys)

        _, u_end, w_end = smooth(R - 1)
        xs, u, w = smooth(0)
        u_top, w_top = u, w
        qu = [pltpu.roll(a, 1, 0) + b for a, b in zip(u_end, u)]
        qw = [pltpu.roll(a, 1, 0) + b for a, b in zip(w_end, w)]
        for c in range(R):
            if c < R - 1:
                x_next, u_next, w_next = smooth(c + 1)
            else:
                x_next = None
                u_next = [pltpu.roll(v, 7, 0) for v in u_top]
                w_next = [pltpu.roll(v, 7, 0) for v in w_top]
            qu2 = [a + b for a, b in zip(u, u_next)]
            qw2 = [a + b for a, b in zip(w, w_next)]
            at = slice(8 * c, 8 * c + 8)
            for t in range(nt):
                pull = SR[t, at, :] * (qu[t] + qu2[t]) + (qw[t] + qw2[t])
                z = rR[t, at, :] * pull + (mR[t, at, :] * xs[t] + spR[t, at, :])
                new = c2 * z - c1 * X[prv, t, at, :]
                if final:
                    xr[t, pl.ds(8 + c, 8, stride=R), :] = new
                else:
                    X[prv, t, at, :] = new
            qu, qw, u, w, xs = qu2, qw2, u_next, w_next, x_next

    @pl.loop(0, (SWEEPS - 2) // 2)
    def _(k):
        sweep(2 * k, 0, 1, False)
        sweep(2 * k + 1, 1, 0, False)

    sweep(SWEEPS - 2, 0, 1, True)

    own0 = 8 + HALO
    best = jnp.zeros((8, 128), F32)
    for c in range(n_rt):
        lo = own0 + 8 * c
        x = [xr[t, lo : lo + 8, :] for t in range(nt)]
        after = x[1:] + [pltpu.roll(x[0], 127, 1)]
        before = [pltpu.roll(x[-1], 1, 1)] + x[:-1]
        for t in range(nt):
            speed = jnp.abs(0.5 * (xr[t, lo + 1 : lo + 9, :] - xr[t, lo - 1 : lo + 7, :]))
            speed = speed + jnp.abs(0.5 * (after[t] - before[t]))
            best = jnp.maximum(best, jnp.where(lane * nt + t < lt * 128, speed, 0.0))
    mx[0:1, :] = jnp.max(best, axis=0, keepdims=True)

    for o, dev in enumerate(others):
        rcopy(mx.at[0:1], mrx.at[o : o + 1], dev, "max", "max").start()

    near = rows + 16
    split_rows(xr, own0 - 8, 0, near)
    moved = jnp.dot(lhs[0:near, :], to_plain[...], preferred_element_type=F32)
    for t in range(lt):
        xn[t, :, :] = moved[:, t * 128 : (t + 1) * 128]
        dnb[t, :, :] = moved[:, (lt + t) * 128 : (lt + t + 1) * 128]
        pot_o[:, t * 128 : (t + 1) * 128] = moved[8 : 8 + rows, t * 128 : (t + 1) * 128]

    from_dn("i_up", ion.at[:, :, 0:8])
    from_up("i_dn", ion.at[:, :, 0:8])

    @pl.loop(0, n_rt, unroll=2)
    def _(c):
        row = pl.multiple_of(8 * c, 8)
        at = pl.ds(row, 8)
        for t in range(lt):
            de = -0.5 * (xn[t, pl.ds(row + 9, 8), :] - xn[t, pl.ds(row + 7, 8), :])
            dv = dnb[t, pl.ds(row + 8, 8), :]
            e_pos, e_neg = jnp.maximum(de, 0.0), jnp.minimum(de, 0.0)
            n_pos, n_neg = jnp.maximum(dv, 0.0), jnp.minimum(dv, 0.0)
            for s in range(3):
                n = ion[s, t, pl.ds(row + 8, 8), :]
                f = e_pos * ion_a[s, t, at, :] + e_neg * ion_b[s, t, at, :]
                f = f + n_pos * (n - ion[s, t, pl.ds(row + 7, 8), :])
                f = f + n_neg * (ion[s, t, pl.ds(row + 9, 8), :] - n)
                flux[s, t, at, :] = f

    arrived("max", mrx.at[0 : n_dev - 1])
    best = jnp.maximum(
        jnp.max(mrx[0 : n_dev - 1, :], axis=0, keepdims=True), mx[0:1, :]
    )
    best = jnp.max(best, axis=1, keepdims=True)
    step = jnp.broadcast_to(COURANT / (best + 1e-6), (8, 128))

    for s in range(3):
        scale = MOBILITY[s] * step

        @pl.loop(0, n_rt, unroll=2)
        def _(c):
            row = pl.multiple_of(8 * c, 8)
            for t in range(lt):
                upd_o[s, pl.ds(row, 8), t * 128 : (t + 1) * 128] = (
                    ion[s, t, pl.ds(row + 8, 8), :] - scale * flux[s, t, pl.ds(row, 8), :]
                )

    to_side = sig.at[:, 0 : 8 + 24 + GUARD + HALO]

    @pl.when(has_up)
    def _():
        sent("up", to_side)

    @pl.when(has_dn)
    def _():
        sent("dn", to_side)

    sent("sig", sig)
    sent("t", t_out)
    sent("lon", pk)
    sent("max", mrx.at[0 : n_dev - 1])


def write_out(pot_v, upd_v, pot_h, upd_h, sem):
    copies = [pltpu.make_async_copy(upd_v.at[s], upd_h.at[s], sem.at[s]) for s in range(3)]
    copies.append(pltpu.make_async_copy(pot_v, pot_h, sem.at[3]))
    for c in copies:
        c.start()
    for c in copies:
        c.wait()


def solution(mesh):
    nlat, nlon = mesh.shape["lat"], mesh.shape["lon"]

    def shards(pedersen, hall_conductivity, east_wind, north_wind, ion_density):
        lev, rows, cols = pedersen.shape
        lt = cols // 128
        nt = lt + 1
        width = nt * 128
        tall = rows + 2 * GUARD
        ext = rows + 2 * HALO
        groups = PIECES + 2
        vm = lambda *shape: pltpu.VMEM(shape, F32)
        half = lambda *shape: pltpu.VMEM(shape, BF16)
        dma = lambda *shape: pltpu.SemaphoreType.DMA(shape)
        hbm = pl.BlockSpec(memory_space=pltpu.HBM)
        vmem = pl.BlockSpec(memory_space=pltpu.VMEM)
        pot, upd = pl.pallas_call(
            functools.partial(kernel, nlat, nlon, lev, rows, lt),
            out_shape=(pltpu.VMEM((rows, cols), F32), pltpu.VMEM((3, rows, cols), F32)),
            in_specs=[hbm] * 5,
            out_specs=(vmem, vmem),
            scratch_shapes=[vm(4, lev, rows, cols)]
            + [vm(3, lt, rows + 16, 128)] + [vm(3, lt, rows, 128)] * 2
            + [vm(lt, rows, 128), vm(lt, rows, 128), vm(lt, rows + 16, 128)]
            + [vm(lt, rows, 128)] * 4
            + [vm(nt, tall, 128)] * 2
            + [vm(4 + 4 * groups, 8, 128)] + [vm(2, 1, 8, 128)] * 2 + [vm(2, groups, 8, 128)] * 2
            + [half(tall, 3 * width), half(3 * width, width), half(3 * width, 2 * lt * 128)]
            + [pltpu.SMEM((2, SWEEPS), F32)]
            + [vm(nt, tall, 128)] * 2
            + [vm(nt, ext, 128)] * 5
            + [vm(2, nt, ext, 128), vm(nt, ext + 16, 128)]
            + [vm(lt, rows + 16, 128)] * 2
            + [vm(3, lt, rows, 128), vm(8, 128), vm(nlat * nlon, 128)]
            + [dma(len(in_groups(rows // 8))), dma(1), dma(len(SEND)), dma(len(RECV))],
            compiler_params=pltpu.CompilerParams(
                collective_id=0, has_side_effects=True, vmem_limit_bytes=60 * 1024 * 1024
            ),
        )(pedersen, hall_conductivity, east_wind, north_wind, ion_density)
        pot = pltpu.with_memory_space_constraint(pot, pltpu.VMEM)
        upd = pltpu.with_memory_space_constraint(upd, pltpu.VMEM)
        return pl.pallas_call(
            write_out,
            out_shape=(
                jax.ShapeDtypeStruct((rows, cols), F32),
                jax.ShapeDtypeStruct((3, rows, cols), F32),
            ),
            in_specs=[vmem, vmem],
            out_specs=(hbm, hbm),
            scratch_shapes=[dma(4)],
        )(pot, upd)

    spec = P(None, "lat", "lon")
    return jax.shard_map(
        shards,
        mesh=mesh,
        in_specs=(spec,) * 5,
        out_specs=(P("lat", "lon"), spec),
        check_vma=False,
    )
```

```python
import functools

import jax
import jax.numpy as jnp
from jax import lax
from jax.experimental import pallas as pl
from jax.experimental.pallas import tpu as pltpu
from jax.sharding import PartitionSpec as P

SWEEPS = 16
DAMPING = 0.0001
LOW_BOUND = 0.05
HIGH_BOUND = 2.0
COURANT = 0.8
MOBILITY = (1.0, 0.6, 0.3)
MESH = pl.DeviceIdType.MESH
GUARD = 24
HALO = 16
PIECES = 4
THETA = 0.5 * (HIGH_BOUND + LOW_BOUND)
F32 = jnp.float32
BF16 = jnp.bfloat16


def chebyshev_factors():
    delta = 0.5 * (HIGH_BOUND - LOW_BOUND)
    sigma_one = THETA / delta
    rho_prev = 1.0 / sigma_one
    first_list = []
    second_list = []
    for sweep in range(SWEEPS):
        rho_next = 1.0 / (2.0 * sigma_one - rho_prev)
        first_list.append(rho_next * rho_prev)
        second_list.append(2.0 * rho_next / delta)
        rho_prev = rho_next
    return first_list, second_list


RECV = ("e", "ion", "n_up", "n_dn", "i_up", "i_dn", "sig_a", "sig_b", "t_a", "t_b", "t_c",
        "s_up", "s_dn", "s_lo", "s_hi", "s_lon", "v_up", "v_dn", "v_lo", "v_hi", "v_lon",
        "inner", "max")
SEND = ("sig", "t", "lon", "up", "dn", "up_lon", "dn_lon", "max")
EDGE = 32


def in_groups(n_rt):
    per = n_rt // PIECES
    spans = [(0, 1), (n_rt - 1, n_rt), (1, per), (n_rt - per, n_rt - 1)]
    for q in range(1, PIECES - 1):
        half = q * per + per // 2
        spans += [(q * per, half), (half, (q + 1) * per)]
    return [p for p in spans if p[1] > p[0]]


def kernel(
    nlat, nlon, lev, rows, lt,
    ped_h, hall_h, east_h, north_h, ion_h,
    pot_o, upd_o,
    vin, ion, ion_a, ion_b,
    sig, cur_e, cur_n, s_one, t_out, sig_rx, t_rx,
    S, src, pk, rx_e, rx_ion, rx_s, rx_v, rx_in,
    lhs, to_strided, to_plain, coef,
    SP, U, SR, rR, mR, invR, spR, X, xr, xn, dnb,
    flux, mx, mrx,
    sem_in, sem_ion, ss, rs,
):
    n_rt = rows // 8
    nt = lt + 1
    width = nt * 128
    R = (rows + 2 * HALO) // 8
    n_dev = nlat * nlon
    me_lat = lax.axis_index("lat")
    me_lon = lax.axis_index("lon")
    has_up = me_lat > 0
    has_dn = me_lat < nlat - 1
    up = (jnp.maximum(me_lat - 1, 0), me_lon)
    dn = (jnp.minimum(me_lat + 1, nlat - 1), me_lon)
    lf = (me_lat, lax.rem(me_lon + nlon - 1, nlon))
    rt = (me_lat, lax.rem(me_lon + 1, nlon))
    mirror = (nlat - 1 - me_lat, me_lon)
    far_lf, far_rt = (mirror[0], lf[1]), (mirror[0], rt[1])
    others = [
        (lax.rem(me_lat + a, nlat), lax.rem(me_lon + b, nlon))
        for a in range(nlat) for b in range(nlon) if a or b
    ]

    barrier = pltpu.get_barrier_semaphore()
    for dev in others:
        pl.semaphore_signal(barrier, inc=1, device_id=dev, device_id_type=MESH)

    per = n_rt // PIECES
    groups = in_groups(n_rt)

    def in_copy(a, g):
        at = slice(8 * groups[g][0], 8 * groups[g][1])
        return pltpu.make_async_copy(
            (ped_h, hall_h, east_h, north_h)[a].at[:, at, :], vin.at[a, :, at, :], sem_in.at[g]
        )

    for g in range(len(groups)):
        for a in range(4):
            in_copy(a, g).start()
    for s in range(3):
        for t in range(lt):
            pltpu.make_async_copy(
                ion_h.at[s, :, t * 128 : (t + 1) * 128], ion.at[s, t, 8 : 8 + rows], sem_ion.at[0]
            ).start()

    first_list, second_list = chebyshev_factors()
    for k in range(SWEEPS):
        coef[0, k] = jnp.float32(first_list[k])
        coef[1, k] = jnp.float32(second_list[k])

    def rcopy(src_ref, dst_ref, dev, send, recv):
        return pltpu.make_async_remote_copy(
            src_ref=src_ref, dst_ref=dst_ref,
            send_sem=ss.at[SEND.index(send)], recv_sem=rs.at[RECV.index(recv)],
            device_id=dev, device_id_type=MESH,
        )

    def arrived(name, view):
        pltpu.make_async_copy(view, view, rs.at[RECV.index(name)]).wait()

    def sent(name, view):
        pltpu.make_async_copy(view, view, ss.at[SEND.index(name)]).wait()

    lane = lax.broadcasted_iota(jnp.int32, (8, 128), 1)
    sub = lax.broadcasted_iota(jnp.int32, (8, 128), 0)

    def turn(v, by):
        by = by % 128
        return pltpu.roll(v, by, 1) if by else v

    def shifts(v, after, before):
        a = [pltpu.roll(t, 1, 1) for t in v]
        b = [pltpu.roll(t, 127, 1) for t in v] + [after]
        left = [jnp.where(lane == 0, p, q) for p, q in zip([before] + a[:-1], a)]
        right = [jnp.where(lane == 127, p, q) for p, q in zip(b[1:], b[:-1])]
        return left, right

    def pack(slot, tiles, step, skip):
        acc = None
        for k, v in enumerate(tiles):
            v = turn(v, step * k + skip)
            acc = v if k == 0 else jnp.where(lane < step * k, acc, v)
        pk[slot, :, :] = acc

    def rev8(v):
        v = pltpu.roll(v, 4, 0)
        for b in (2, 1):
            v = jnp.where((sub & b) == 0, pltpu.roll(v, 8 - b, 0), pltpu.roll(v, b, 0))
        return v

    @pl.loop(0, width // 16, unroll=4)
    def _(c):
        row = lax.broadcasted_iota(jnp.int32, (16, 128), 0) + 16 * c
        col = lax.broadcasted_iota(jnp.int32, (16, 128), 1)
        for t in range(nt):
            there = jnp.where(row == col * nt + t, 1.0, 0.0).astype(BF16)
            for part in range(3):
                at = pl.ds(pl.multiple_of(part * width + 16 * c, 16), 16)
                to_strided[at, t * 128 : (t + 1) * 128] = there

    weight = [(0.5 + l / lev) / lev for l in range(lev)]

    def columns(g):
        lo, hi = groups[g]
        view = vin.at[:, :, 8 * lo : 8 * hi, :]
        pltpu.make_async_copy(view, view, sem_in.at[g]).wait()

        @pl.loop(lo, hi)
        def _(c):
            row = pl.multiple_of(8 * c, 8)
            for t in range(lt):
                at = (pl.ds(row, 8), slice(t * 128, (t + 1) * 128))
                acc = [jnp.zeros((8, 128), F32)] * 3
                for l in range(lev):
                    p, h = weight[l] * vin[(0, l) + at], weight[l] * vin[(1, l) + at]
                    e, n = vin[(2, l) + at], vin[(3, l) + at]
                    acc = [acc[0] + p, acc[1] + (p * e + h * n), acc[2] + (p * n - h * e)]
                sig[t, pl.ds(row, 8), :] = acc[0]
                cur_e[t, pl.ds(row, 8), :] = acc[1]
                cur_n[t, pl.ds(row + 8, 8), :] = acc[2]

    def band(q):
        return slice(q * per * 8, (q + 1) * per * 8)

    def send_sig(q, recv):
        rcopy(sig.at[:, band(q)], sig_rx.at[:, band(q)], mirror, "sig", recv).start()

    def send_t(q, recv):
        rcopy(t_out.at[:, band(q)], t_rx.at[:, band(q)], mirror, "t", recv).start()

    def to_up(src_ref, dst_ref, recv):
        @pl.when(has_up)
        def _():
            rcopy(src_ref, dst_ref, up, "up", recv).start()

    def to_dn(src_ref, dst_ref, recv):
        @pl.when(has_dn)
        def _():
            rcopy(src_ref, dst_ref, dn, "dn", recv).start()

    def from_dn(name, view):
        @pl.when(has_dn)
        def _():
            arrived(name, view)

    def from_up(name, view):
        @pl.when(has_up)
        def _():
            arrived(name, view)

    def send_lon(slot, rx, g, recv):
        rcopy(pk.at[slot], rx.at[0, g], lf, "lon", recv).start()
        rcopy(pk.at[slot + 1], rx.at[1, g], rt, "lon", recv).start()

    columns(0)
    columns(1)
    pl.semaphore_wait(barrier, n_dev - 1)
    to_up(cur_n.at[:, 8:16], cur_n.at[:, rows + 8 : rows + 16], "n_up")
    to_dn(cur_n.at[:, rows : rows + 8], cur_n.at[:, 0:8], "n_dn")
    columns(2)
    send_sig(0, "sig_a")
    columns(3)
    send_sig(PIECES - 1, "sig_a")
    for q in range(1, PIECES - 1):
        columns(2 * q + 2)
        columns(2 * q + 3)
        send_sig(q, "sig_b")

    step_e = 128 // n_rt
    pack(0, [cur_e[0, 8 * c : 8 * c + 8, :] for c in range(n_rt)], step_e, 0)
    pack(1, [cur_e[lt - 1, 8 * c : 8 * c + 8, :] for c in range(n_rt)], step_e, 1)
    send_lon(0, rx_e, 0, "e")

    @pl.when(jnp.logical_not(has_up))
    def _():
        cur_n[:, 0:8, :] = jnp.zeros((lt, 8, 128), F32)
        ion[:, :, 0:8, :] = jnp.zeros((3, lt, 8, 128), F32)
        S[:, 0:GUARD, :] = jnp.zeros((nt, GUARD, 128), F32)
        src[:, 0:GUARD, :] = jnp.zeros((nt, GUARD, 128), F32)

    @pl.when(jnp.logical_not(has_dn))
    def _():
        cur_n[:, rows + 8 : rows + 16, :] = jnp.zeros((lt, 8, 128), F32)
        ion[:, :, rows + 8 : rows + 16, :] = jnp.zeros((3, lt, 8, 128), F32)
        S[:, GUARD + rows :, :] = jnp.zeros((nt, GUARD, 128), F32)
        src[:, GUARD + rows :, :] = jnp.zeros((nt, GUARD, 128), F32)

    view = ion.at[:, :, 8 : 8 + rows]
    pltpu.make_async_copy(view, view, sem_ion.at[0]).wait()
    step_i = 128 // (3 * n_rt)
    bands = [(s, c) for s in range(3) for c in range(n_rt)]
    pack(2, [ion[s, 0, 8 * c + 8 : 8 * c + 16, :] for s, c in bands], step_i, 0)
    pack(3, [ion[s, lt - 1, 8 * c + 8 : 8 * c + 16, :] for s, c in bands], step_i, 1)
    send_lon(2, rx_ion, 0, "ion")

    from_dn("n_up", cur_n.at[:, 0:8])
    from_up("n_dn", cur_n.at[:, 0:8])
    arrived("e", rx_e)
    e_fr, e_fl = rx_e[0, 0, :, :], rx_e[1, 0, :, :]
    for q in [0, PIECES - 1] + list(range(1, PIECES - 1)):
        for c in range(q * per, (q + 1) * per):
            row = 8 * c
            at = slice(row, row + 8)
            left, right = shifts(
                [cur_e[t, at, :] for t in range(lt)],
                turn(e_fr, 127 - step_e * c), turn(e_fl, 128 - step_e * c),
            )
            for t in range(lt):
                d_lon = 0.5 * (right[t] - left[t])
                d_lat = 0.5 * (cur_n[t, row + 9 : row + 17, :] - cur_n[t, row + 7 : row + 15, :])
                s_one[t, at, :] = d_lon + d_lat
                t_out[t, at, :] = d_lon - d_lat

    outer, inner = [0, PIECES - 1], list(range(1, PIECES - 1))
    slot_s = 4
    slot_v = slot_s + 2 * PIECES
    slot_in = slot_v + 2 * len(outer)
    slot_far = slot_in + 2 * len(inner)
    slot_corner = slot_far + 2 * len(inner)
    for i, q in enumerate(inner):
        home = [8 * (q * per + k) for k in range(per)]
        for side, t in enumerate((0, lt - 1)):
            near_slot, far_slot = slot_in + 2 * i + side, slot_far + 2 * i + side
            pack(near_slot, [s_one[t, r : r + 8, :] for r in home], EDGE, side * EDGE)
            pack(far_slot, [t_out[t, r : r + 8, :] for r in home[::-1]], EDGE, side * EDGE)
            there, mine = len(inner) - 1 - i, i
            rcopy(pk.at[near_slot], rx_in.at[side, 0, mine], (lf, rt)[side], "lon", "inner").start()
            rcopy(
                pk.at[far_slot], rx_in.at[side, 1, there], (far_lf, far_rt)[side], "lon", "inner"
            ).start()

    for j in range(nt):
        @pl.loop(0, 8, unroll=2)
        def _(c):
            row = lax.broadcasted_iota(jnp.int32, (16, 128), 0) + 16 * c
            col = lax.broadcasted_iota(jnp.int32, (16, 128), 1)
            home = row * nt + j
            for t in range(lt):
                here = col + t * 128
                back = jnp.where(home == here, 1.0, 0.0).astype(BF16)
                before = jnp.where(here == 0, width - 1, here - 1)
                slope = jnp.where(
                    home == here + 1, 0.5, jnp.where(home == before, -0.5, 0.0)
                ).astype(BF16)
                for part in range(3):
                    at = pl.ds(pl.multiple_of(part * width + j * 128 + 16 * c, 16), 16)
                    to_plain[at, t * 128 : (t + 1) * 128] = back
                    to_plain[at, (lt + t) * 128 : (lt + t + 1) * 128] = slope

    def combine(own, rx, out, q):
        p = PIECES - 1 - q
        for c in range(p * per, (p + 1) * per):
            back = rows - 8 - 8 * c
            for t in range(lt):
                out[t, 8 * c + GUARD : 8 * c + GUARD + 8, :] = own[
                    t, 8 * c : 8 * c + 8, :
                ] + rev8(rx[t, back : back + 8, :])

    def spread(out, rx, slot, g, lo, count, recv):
        tiles = lambda t: [out[t, lo + 8 * k : lo + 8 * k + 8, :] for k in range(count)]
        pack(slot, tiles(0), EDGE, 0)
        pack(slot + 1, tiles(lt - 1), EDGE, EDGE)
        send_lon(slot, rx, g, recv)

    def gather(out, rx, g, lo, count):
        fr, fl = rx[0, g, :, :], rx[1, g, :, :]
        for k in range(count):
            a, b = turn(fr, 128 - EDGE * k), turn(fl, 256 - EDGE - EDGE * k)
            out[lt, lo + 8 * k : lo + 8 * k + 8, :] = jnp.where(
                lane < EDGE, a, jnp.where(lane >= 128 - EDGE, b, 0.0)
            )

    def spread_piece(out, rx, slot, q, recv):
        p = PIECES - 1 - q
        spread(out, rx, slot, p, GUARD + p * per * 8, per, recv)

    def gather_piece(out, rx, q):
        p = PIECES - 1 - q
        gather(out, rx, p, GUARD + p * per * 8, per)

    def lat_send(out, rx, depth, name, slot):
        lo, hi = GUARD, GUARD + rows
        to_up(out.at[0:lt, lo : lo + depth], out.at[0:lt, hi : hi + depth], name + "_up")
        to_dn(out.at[0:lt, hi - depth : hi], out.at[0:lt, lo - depth : lo], name + "_dn")
        for edge, first in enumerate((lo, hi - depth)):
            for side, t in enumerate((0, lt - 1)):
                tiles = [out[t, r : r + 8, :] for r in range(first, first + depth, 8)]
                pack(slot + 2 * edge + side, tiles, EDGE, side * EDGE)

        def corners(edge, lat, send, recv):
            for side, lon in enumerate((lf[1], rt[1])):
                rcopy(
                    pk.at[slot + 2 * edge + side], rx.at[side, PIECES + 1 - edge], (lat, lon),
                    send, recv,
                ).start()

        @pl.when(has_up)
        def _():
            corners(0, up[0], "up_lon", name + "_hi")

        @pl.when(has_dn)
        def _():
            corners(1, dn[0], "dn_lon", name + "_lo")

    def lat_gather(out, rx, depth, name):
        lo, hi = GUARD, GUARD + rows

        @pl.when(has_up)
        def _():
            arrived(name + "_dn", out.at[0:lt, lo - depth : lo])
            arrived(name + "_lo", pk.at[0:2])
            gather(out, rx, PIECES, lo - depth, depth // 8)

        @pl.when(has_dn)
        def _():
            arrived(name + "_up", out.at[0:lt, lo - depth : lo])
            arrived(name + "_hi", pk.at[0:2])
            gather(out, rx, PIECES + 1, hi, depth // 8)

    arrived("sig_a", sig_rx.at[:, 0 : 2 * per * 8])
    for q in outer:
        combine(sig, sig_rx, S, q)
    lat_send(S, rx_s, GUARD, "s", slot_corner)
    for q in outer:
        send_t(q, "t_a")
    for q in inner[:-1]:
        send_t(q, "t_b")
    for i, q in enumerate(outer):
        spread_piece(S, rx_s, slot_s + 2 * i, q, "s_lon")
    arrived("sig_b", sig_rx.at[:, 0 : (PIECES - 2) * per * 8])
    for i, q in enumerate(inner):
        combine(sig, sig_rx, S, q)
        spread_piece(S, rx_s, slot_s + 4 + 2 * i, q, "s_lon")

    arrived("ion", rx_ion)
    i_fr, i_fl = rx_ion[0, 0, :, :], rx_ion[1, 0, :, :]
    for k, (s, c) in enumerate(bands):
        at = slice(8 * c, 8 * c + 8)
        tiles = [ion[s, t, 8 * c + 8 : 8 * c + 16, :] for t in range(lt)]
        left, right = shifts(tiles, turn(i_fr, 127 - step_i * k), turn(i_fl, 128 - step_i * k))
        for t in range(lt):
            ion_a[s, t, at, :] = tiles[t] - left[t]
            ion_b[s, t, at, :] = right[t] - tiles[t]

    arrived("t_a", t_rx.at[:, 0 : 2 * per * 8])
    for q in outer:
        combine(s_one, t_rx, src, q)
    lat_send(src, rx_v, HALO, "v", slot_corner + 4)
    send_t(inner[-1], "t_c")
    to_up(ion.at[:, :, 8:16], ion.at[:, :, rows + 8 : rows + 16], "i_up")
    to_dn(ion.at[:, :, rows : rows + 8], ion.at[:, :, 0:8], "i_dn")
    for i, q in enumerate(outer):
        spread_piece(src, rx_v, slot_v + 2 * i, q, "v_lon")

    arrived("s_lon", rx_s.at[:, 0:PIECES])
    for q in outer + inner:
        gather_piece(S, rx_s, q)
    lat_gather(S, rx_s, GUARD, "s")

    def split(v, at, t):
        for part in range(3):
            low = v.astype(BF16)
            lhs[at, part * width + t * 128 : part * width + (t + 1) * 128] = low
            v = v - low.astype(F32)

    def split_rows(ref, first, lo, hi):
        for row in range(lo, hi, 16):
            for t in range(nt):
                split(ref[t, row + first : row + first + 16, :], slice(row, row + 16), t)

    def conv_lon(v):
        after = v[1:] + [pltpu.roll(v[0], 127, 1)]
        p = [a + b for a, b in zip(v, after)]
        before = [pltpu.roll(p[-1], 1, 1)] + p[:-1]
        return [a + b for a, b in zip(p, before)]

    tall = rows + 2 * GUARD
    ext = rows + 2 * HALO
    split_rows(S, 0, 0, tall)
    moved = jnp.dot(lhs[0:tall, :], to_strided[...], preferred_element_type=F32)
    for t in range(nt):
        SP[t, :, :] = moved[:, t * 128 : (t + 1) * 128]

    for c in range(tall // 8):
        for t, v in enumerate(conv_lon([SP[t, 8 * c : 8 * c + 8, :] for t in range(nt)])):
            U[t, 8 * c : 8 * c + 8, :] = v

    total = rows * nlat
    skip = GUARD - HALO
    for c in range(R):
        where = sub * R + (c - HALO + me_lat * rows)
        inside = (where >= 0) & (where < total)
        at = slice(8 * c, 8 * c + 8)
        for t in range(nt):
            s = SP[t, pl.ds(skip + c, 8, stride=R), :]
            around = U[t, pl.ds(skip + c - 1, 8, stride=R), :] + U[
                t, pl.ds(skip + c + 1, 8, stride=R), :
            ]
            around = around + 2.0 * U[t, pl.ds(skip + c, 8, stride=R), :]
            inv = jnp.where(inside, 1.0 / (DAMPING + 2.0 * s + 0.25 * around), 0.0)
            quarter = 0.25 * inv
            SR[t, at, :] = s
            invR[t, at, :] = inv
            rR[t, at, :] = quarter
            mR[t, at, :] = (THETA - 1.0) - 8.0 * (quarter * s)
            X[1, t, at, :] = jnp.zeros((8, 128), F32)

    def inner_edges(q):
        p = PIECES - 1 - q
        for side in range(2):
            rx_v[side, p, :, :] = rx_in[side, 0, p - 1, :, :] + rev8(rx_in[side, 1, p - 1, :, :])
        gather_piece(src, rx_v, q)

    arrived("t_b", t_rx.at[:, 0 : (PIECES - 3) * per * 8])
    for q in inner[:-1]:
        combine(s_one, t_rx, src, q)
    arrived("inner", rx_in)
    for q in inner:
        inner_edges(q)
    arrived("v_lon", pk.at[0 : 2 * len(outer)])
    for q in outer:
        gather_piece(src, rx_v, q)
    lat_gather(src, rx_v, HALO, "v")
    last = PIECES - 1 - inner[-1]
    last_lo, last_hi = HALO + last * per * 8, HALO + (last + 1) * per * 8
    for lo, hi in ((0, last_lo), (last_hi, ext)):
        split_rows(src, skip, lo, hi)
        moved = jnp.dot(lhs[lo:hi, :], to_strided[...], preferred_element_type=F32)
        for t in range(nt):
            SP[t, lo:hi, :] = moved[:, t * 128 : (t + 1) * 128]

    arrived("t_c", t_rx.at[:, 0 : per * 8])
    combine(s_one, t_rx, src, inner[-1])
    split_rows(src, skip, last_lo, last_hi)
    moved = jnp.dot(lhs[last_lo:last_hi, :], to_strided[...], preferred_element_type=F32)
    for t in range(nt):
        SP[t, last_lo:last_hi, :] = moved[:, t * 128 : (t + 1) * 128]
    for c in range(R):
        at = slice(8 * c, 8 * c + 8)
        for t in range(nt):
            first = SP[t, pl.ds(c, 8, stride=R), :] * invR[t, at, :]
            spR[t, at, :] = first
            X[0, t, at, :] = first * (1.0 / THETA)

    def sweep(k, cur, prv, final):
        c1 = coef[0, k]
        c2 = coef[1, k]

        def smooth(c):
            at = slice(8 * c, 8 * c + 8)
            xs = [X[cur, t, at, :] for t in range(nt)]
            ys = [SR[t, at, :] * xs[t] for t in range(nt)]
            return xs, conv_lon(xs), conv_lon(ys)

        _, u_end, w_end = smooth(R - 1)
        xs, u, w = smooth(0)
        u_top, w_top = u, w
        qu = [pltpu.roll(a, 1, 0) + b for a, b in zip(u_end, u)]
        qw = [pltpu.roll(a, 1, 0) + b for a, b in zip(w_end, w)]
        for c in range(R):
            if c < R - 1:
                x_next, u_next, w_next = smooth(c + 1)
            else:
                x_next = None
                u_next = [pltpu.roll(v, 7, 0) for v in u_top]
                w_next = [pltpu.roll(v, 7, 0) for v in w_top]
            qu2 = [a + b for a, b in zip(u, u_next)]
            qw2 = [a + b for a, b in zip(w, w_next)]
            at = slice(8 * c, 8 * c + 8)
            for t in range(nt):
                pull = SR[t, at, :] * (qu[t] + qu2[t]) + (qw[t] + qw2[t])
                z = rR[t, at, :] * pull + (mR[t, at, :] * xs[t] + spR[t, at, :])
                new = c2 * z - c1 * X[prv, t, at, :]
                if final:
                    xr[t, pl.ds(8 + c, 8, stride=R), :] = new
                else:
                    X[prv, t, at, :] = new
            qu, qw, u, w, xs = qu2, qw2, u_next, w_next, x_next

    @pl.loop(0, (SWEEPS - 2) // 2)
    def _(k):
        sweep(2 * k, 0, 1, False)
        sweep(2 * k + 1, 1, 0, False)

    sweep(SWEEPS - 2, 0, 1, True)

    own0 = 8 + HALO
    best = jnp.zeros((8, 128), F32)
    for c in range(n_rt):
        lo = own0 + 8 * c
        x = [xr[t, lo : lo + 8, :] for t in range(nt)]
        after = x[1:] + [pltpu.roll(x[0], 127, 1)]
        before = [pltpu.roll(x[-1], 1, 1)] + x[:-1]
        for t in range(nt):
            speed = jnp.abs(0.5 * (xr[t, lo + 1 : lo + 9, :] - xr[t, lo - 1 : lo + 7, :]))
            speed = speed + jnp.abs(0.5 * (after[t] - before[t]))
            best = jnp.maximum(best, jnp.where(lane * nt + t < lt * 128, speed, 0.0))
    mx[0:1, :] = jnp.max(best, axis=0, keepdims=True)

    for o, dev in enumerate(others):
        rcopy(mx.at[0:1], mrx.at[o : o + 1], dev, "max", "max").start()

    near = rows + 16
    split_rows(xr, own0 - 8, 0, near)
    moved = jnp.dot(lhs[0:near, :], to_plain[...], preferred_element_type=F32)
    for t in range(lt):
        xn[t, :, :] = moved[:, t * 128 : (t + 1) * 128]
        dnb[t, :, :] = moved[:, (lt + t) * 128 : (lt + t + 1) * 128]
        pot_o[:, t * 128 : (t + 1) * 128] = moved[8 : 8 + rows, t * 128 : (t + 1) * 128]

    from_dn("i_up", ion.at[:, :, 0:8])
    from_up("i_dn", ion.at[:, :, 0:8])

    @pl.loop(0, n_rt, unroll=2)
    def _(c):
        row = pl.multiple_of(8 * c, 8)
        at = pl.ds(row, 8)
        for t in range(lt):
            de = -0.5 * (xn[t, pl.ds(row + 9, 8), :] - xn[t, pl.ds(row + 7, 8), :])
            dv = dnb[t, pl.ds(row + 8, 8), :]
            e_pos, e_neg = jnp.maximum(de, 0.0), jnp.minimum(de, 0.0)
            n_pos, n_neg = jnp.maximum(dv, 0.0), jnp.minimum(dv, 0.0)
            for s in range(3):
                n = ion[s, t, pl.ds(row + 8, 8), :]
                f = e_pos * ion_a[s, t, at, :] + e_neg * ion_b[s, t, at, :]
                f = f + n_pos * (n - ion[s, t, pl.ds(row + 7, 8), :])
                f = f + n_neg * (ion[s, t, pl.ds(row + 9, 8), :] - n)
                flux[s, t, at, :] = f

    arrived("max", mrx.at[0 : n_dev - 1])
    best = jnp.maximum(
        jnp.max(mrx[0 : n_dev - 1, :], axis=0, keepdims=True), mx[0:1, :]
    )
    best = jnp.max(best, axis=1, keepdims=True)
    step = jnp.broadcast_to(COURANT / (best + 1e-6), (8, 128))

    for s in range(3):
        scale = MOBILITY[s] * step

        @pl.loop(0, n_rt, unroll=2)
        def _(c):
            row = pl.multiple_of(8 * c, 8)
            for t in range(lt):
                upd_o[s, pl.ds(row, 8), t * 128 : (t + 1) * 128] = (
                    ion[s, t, pl.ds(row + 8, 8), :] - scale * flux[s, t, pl.ds(row, 8), :]
                )

    to_side = sig.at[:, 0 : 8 + 24 + GUARD + HALO]

    @pl.when(has_up)
    def _():
        sent("up", to_side)
        sent("up_lon", pk.at[0:4])

    @pl.when(has_dn)
    def _():
        sent("dn", to_side)
        sent("dn_lon", pk.at[0:4])

    sent("sig", sig)
    sent("t", t_out)
    sent("lon", pk.at[0:slot_corner])
    sent("max", mrx.at[0 : n_dev - 1])


def write_out(pot_v, upd_v, pot_h, upd_h, sem):
    copies = [pltpu.make_async_copy(upd_v.at[s], upd_h.at[s], sem.at[s]) for s in range(3)]
    copies.append(pltpu.make_async_copy(pot_v, pot_h, sem.at[3]))
    for c in copies:
        c.start()
    for c in copies:
        c.wait()


def solution(mesh):
    nlat, nlon = mesh.shape["lat"], mesh.shape["lon"]

    def shards(pedersen, hall_conductivity, east_wind, north_wind, ion_density):
        lev, rows, cols = pedersen.shape
        lt = cols // 128
        nt = lt + 1
        width = nt * 128
        tall = rows + 2 * GUARD
        ext = rows + 2 * HALO
        groups = PIECES + 2
        vm = lambda *shape: pltpu.VMEM(shape, F32)
        half = lambda *shape: pltpu.VMEM(shape, BF16)
        dma = lambda *shape: pltpu.SemaphoreType.DMA(shape)
        hbm = pl.BlockSpec(memory_space=pltpu.HBM)
        vmem = pl.BlockSpec(memory_space=pltpu.VMEM)
        pot, upd = pl.pallas_call(
            functools.partial(kernel, nlat, nlon, lev, rows, lt),
            out_shape=(pltpu.VMEM((rows, cols), F32), pltpu.VMEM((3, rows, cols), F32)),
            in_specs=[hbm] * 5,
            out_specs=(vmem, vmem),
            scratch_shapes=[vm(4, lev, rows, cols)]
            + [vm(3, lt, rows + 16, 128)] + [vm(3, lt, rows, 128)] * 2
            + [vm(lt, rows, 128), vm(lt, rows, 128), vm(lt, rows + 16, 128)]
            + [vm(lt, rows, 128)] * 4
            + [vm(nt, tall, 128)] * 2
            + [vm(8 * PIECES, 8, 128)] + [vm(2, 1, 8, 128)] * 2 + [vm(2, groups, 8, 128)] * 2
            + [vm(2, 2, PIECES - 2, 8, 128)]
            + [half(tall, 3 * width), half(3 * width, width), half(3 * width, 2 * lt * 128)]
            + [pltpu.SMEM((2, SWEEPS), F32)]
            + [vm(nt, tall, 128)] * 2
            + [vm(nt, ext, 128)] * 5
            + [vm(2, nt, ext, 128), vm(nt, ext + 16, 128)]
            + [vm(lt, rows + 16, 128)] * 2
            + [vm(3, lt, rows, 128), vm(8, 128), vm(nlat * nlon, 128)]
            + [dma(len(in_groups(rows // 8))), dma(1), dma(len(SEND)), dma(len(RECV))],
            compiler_params=pltpu.CompilerParams(
                collective_id=0, has_side_effects=True, vmem_limit_bytes=60 * 1024 * 1024
            ),
        )(pedersen, hall_conductivity, east_wind, north_wind, ion_density)
        pot = pltpu.with_memory_space_constraint(pot, pltpu.VMEM)
        upd = pltpu.with_memory_space_constraint(upd, pltpu.VMEM)
        return pl.pallas_call(
            write_out,
            out_shape=(
                jax.ShapeDtypeStruct((rows, cols), F32),
                jax.ShapeDtypeStruct((3, rows, cols), F32),
            ),
            in_specs=[vmem, vmem],
            out_specs=(hbm, hbm),
            scratch_shapes=[dma(4)],
        )(pot, upd)

    spec = P(None, "lat", "lon")
    return jax.shard_map(
        shards,
        mesh=mesh,
        in_specs=(spec,) * 5,
        out_specs=(P("lat", "lon"), spec),
        check_vma=False,
    )
```

```python
import functools

import jax
import jax.numpy as jnp
from jax import lax
from jax.experimental import pallas as pl
from jax.experimental.pallas import tpu as pltpu
from jax.sharding import PartitionSpec as P

SWEEPS = 16
DAMPING = 0.0001
LOW_BOUND = 0.05
HIGH_BOUND = 2.0
COURANT = 0.8
MOBILITY = (1.0, 0.6, 0.3)
MESH = pl.DeviceIdType.MESH
GUARD = 24
HALO = 16
PIECES = 4
THETA = 0.5 * (HIGH_BOUND + LOW_BOUND)
F32 = jnp.float32
BF16 = jnp.bfloat16


def chebyshev_factors():
    delta = 0.5 * (HIGH_BOUND - LOW_BOUND)
    sigma_one = THETA / delta
    rho_prev = 1.0 / sigma_one
    first_list = []
    second_list = []
    for sweep in range(SWEEPS):
        rho_next = 1.0 / (2.0 * sigma_one - rho_prev)
        first_list.append(rho_next * rho_prev)
        second_list.append(2.0 * rho_next / delta)
        rho_prev = rho_next
    return first_list, second_list


RECV = ("e", "ion", "n_up", "n_dn", "i_up", "i_dn", "sig_a", "sig_b", "t_a", "t_b", "t_c",
        "s_up", "s_dn", "s_lo", "s_hi", "s_lon", "v_up", "v_dn", "v_lo", "v_hi", "v_lon",
        "inner", "inner_s", "max")
SEND = ("sig", "t", "lon", "up", "dn", "up_lon", "dn_lon", "max")
EDGE = 32


def in_groups(n_rt):
    per = n_rt // PIECES
    spans = [(0, 1), (n_rt - 1, n_rt), (1, per), (n_rt - per, n_rt - 1)]
    for q in range(1, PIECES - 1):
        half = q * per + per // 2
        spans += [(q * per, half), (half, (q + 1) * per)]
    return [p for p in spans if p[1] > p[0]]


def kernel(
    nlat, nlon, lev, rows, lt,
    ped_h, hall_h, east_h, north_h, ion_h,
    pot_o, upd_o,
    vin, ion, ion_a, ion_b,
    sig, cur_e, cur_n, s_one, t_out, sig_rx, t_rx,
    S, src, pk, rx_e, rx_ion, rx_s, rx_v, rx_in, rx_ins,
    lhs, to_strided, to_plain, coef,
    SP, U, SR, rR, mR, invR, spR, X, xr, xn, dnb,
    flux, mx, mrx,
    sem_in, sem_ion, ss, rs,
):
    n_rt = rows // 8
    nt = lt + 1
    width = nt * 128
    R = (rows + 2 * HALO) // 8
    n_dev = nlat * nlon
    me_lat = lax.axis_index("lat")
    me_lon = lax.axis_index("lon")
    has_up = me_lat > 0
    has_dn = me_lat < nlat - 1
    up = (jnp.maximum(me_lat - 1, 0), me_lon)
    dn = (jnp.minimum(me_lat + 1, nlat - 1), me_lon)
    lf = (me_lat, lax.rem(me_lon + nlon - 1, nlon))
    rt = (me_lat, lax.rem(me_lon + 1, nlon))
    mirror = (nlat - 1 - me_lat, me_lon)
    far_lf, far_rt = (mirror[0], lf[1]), (mirror[0], rt[1])
    others = [
        (lax.rem(me_lat + a, nlat), lax.rem(me_lon + b, nlon))
        for a in range(nlat) for b in range(nlon) if a or b
    ]

    barrier = pltpu.get_barrier_semaphore()
    for dev in others:
        pl.semaphore_signal(barrier, inc=1, device_id=dev, device_id_type=MESH)

    per = n_rt // PIECES
    groups = in_groups(n_rt)

    def in_copy(a, g):
        at = slice(8 * groups[g][0], 8 * groups[g][1])
        return pltpu.make_async_copy(
            (ped_h, hall_h, east_h, north_h)[a].at[:, at, :], vin.at[a, :, at, :], sem_in.at[g]
        )

    for g in range(len(groups)):
        for a in range(4):
            in_copy(a, g).start()
    for s in range(3):
        for t in range(lt):
            pltpu.make_async_copy(
                ion_h.at[s, :, t * 128 : (t + 1) * 128], ion.at[s, t, 8 : 8 + rows], sem_ion.at[0]
            ).start()

    first_list, second_list = chebyshev_factors()
    for k in range(SWEEPS):
        coef[0, k] = jnp.float32(first_list[k])
        coef[1, k] = jnp.float32(second_list[k])

    def rcopy(src_ref, dst_ref, dev, send, recv):
        return pltpu.make_async_remote_copy(
            src_ref=src_ref, dst_ref=dst_ref,
            send_sem=ss.at[SEND.index(send)], recv_sem=rs.at[RECV.index(recv)],
            device_id=dev, device_id_type=MESH,
        )

    def arrived(name, view):
        pltpu.make_async_copy(view, view, rs.at[RECV.index(name)]).wait()

    def sent(name, view):
        pltpu.make_async_copy(view, view, ss.at[SEND.index(name)]).wait()

    lane = lax.broadcasted_iota(jnp.int32, (8, 128), 1)
    sub = lax.broadcasted_iota(jnp.int32, (8, 128), 0)

    def turn(v, by):
        by = by % 128
        return pltpu.roll(v, by, 1) if by else v

    def shifts(v, after, before):
        a = [pltpu.roll(t, 1, 1) for t in v]
        b = [pltpu.roll(t, 127, 1) for t in v] + [after]
        left = [jnp.where(lane == 0, p, q) for p, q in zip([before] + a[:-1], a)]
        right = [jnp.where(lane == 127, p, q) for p, q in zip(b[1:], b[:-1])]
        return left, right

    def pack(slot, tiles, step, skip):
        acc = None
        for k, v in enumerate(tiles):
            v = turn(v, step * k + skip)
            acc = v if k == 0 else jnp.where(lane < step * k, acc, v)
        pk[slot, :, :] = acc

    def rev8(v):
        v = pltpu.roll(v, 4, 0)
        for b in (2, 1):
            v = jnp.where((sub & b) == 0, pltpu.roll(v, 8 - b, 0), pltpu.roll(v, b, 0))
        return v

    @pl.loop(0, width // 16, unroll=4)
    def _(c):
        row = lax.broadcasted_iota(jnp.int32, (16, 128), 0) + 16 * c
        col = lax.broadcasted_iota(jnp.int32, (16, 128), 1)
        for t in range(nt):
            there = jnp.where(row == col * nt + t, 1.0, 0.0).astype(BF16)
            for part in range(3):
                at = pl.ds(pl.multiple_of(part * width + 16 * c, 16), 16)
                to_strided[at, t * 128 : (t + 1) * 128] = there

    weight = [(0.5 + l / lev) / lev for l in range(lev)]

    def columns(g):
        lo, hi = groups[g]
        view = vin.at[:, :, 8 * lo : 8 * hi, :]
        pltpu.make_async_copy(view, view, sem_in.at[g]).wait()

        @pl.loop(lo, hi)
        def _(c):
            row = pl.multiple_of(8 * c, 8)
            for t in range(lt):
                at = (pl.ds(row, 8), slice(t * 128, (t + 1) * 128))
                acc = [jnp.zeros((8, 128), F32)] * 3
                for l in range(lev):
                    p, h = weight[l] * vin[(0, l) + at], weight[l] * vin[(1, l) + at]
                    e, n = vin[(2, l) + at], vin[(3, l) + at]
                    acc = [acc[0] + p, acc[1] + (p * e + h * n), acc[2] + (p * n - h * e)]
                sig[t, pl.ds(row, 8), :] = acc[0]
                cur_e[t, pl.ds(row, 8), :] = acc[1]
                cur_n[t, pl.ds(row + 8, 8), :] = acc[2]

    def band(q):
        return slice(q * per * 8, (q + 1) * per * 8)

    def send_sig(q, recv):
        rcopy(sig.at[:, band(q)], sig_rx.at[:, band(q)], mirror, "sig", recv).start()

    def send_t(q, recv):
        rcopy(t_out.at[:, band(q)], t_rx.at[:, band(q)], mirror, "t", recv).start()

    def to_up(src_ref, dst_ref, recv):
        @pl.when(has_up)
        def _():
            rcopy(src_ref, dst_ref, up, "up", recv).start()

    def to_dn(src_ref, dst_ref, recv):
        @pl.when(has_dn)
        def _():
            rcopy(src_ref, dst_ref, dn, "dn", recv).start()

    def from_dn(name, view):
        @pl.when(has_dn)
        def _():
            arrived(name, view)

    def from_up(name, view):
        @pl.when(has_up)
        def _():
            arrived(name, view)

    def send_lon(slot, rx, g, recv):
        rcopy(pk.at[slot], rx.at[0, g], lf, "lon", recv).start()
        rcopy(pk.at[slot + 1], rx.at[1, g], rt, "lon", recv).start()

    columns(0)
    columns(1)
    pl.semaphore_wait(barrier, n_dev - 1)
    to_up(cur_n.at[:, 8:16], cur_n.at[:, rows + 8 : rows + 16], "n_up")
    to_dn(cur_n.at[:, rows : rows + 8], cur_n.at[:, 0:8], "n_dn")
    columns(2)
    send_sig(0, "sig_a")
    columns(3)
    send_sig(PIECES - 1, "sig_a")
    for q in range(1, PIECES - 1):
        columns(2 * q + 2)
        columns(2 * q + 3)

    step_e = 128 // n_rt
    pack(0, [cur_e[0, 8 * c : 8 * c + 8, :] for c in range(n_rt)], step_e, 0)
    pack(1, [cur_e[lt - 1, 8 * c : 8 * c + 8, :] for c in range(n_rt)], step_e, 1)
    send_lon(0, rx_e, 0, "e")

    @pl.when(jnp.logical_not(has_up))
    def _():
        cur_n[:, 0:8, :] = jnp.zeros((lt, 8, 128), F32)
        ion[:, :, 0:8, :] = jnp.zeros((3, lt, 8, 128), F32)
        S[:, 0:GUARD, :] = jnp.zeros((nt, GUARD, 128), F32)
        src[:, 0:GUARD, :] = jnp.zeros((nt, GUARD, 128), F32)

    @pl.when(jnp.logical_not(has_dn))
    def _():
        cur_n[:, rows + 8 : rows + 16, :] = jnp.zeros((lt, 8, 128), F32)
        ion[:, :, rows + 8 : rows + 16, :] = jnp.zeros((3, lt, 8, 128), F32)
        S[:, GUARD + rows :, :] = jnp.zeros((nt, GUARD, 128), F32)
        src[:, GUARD + rows :, :] = jnp.zeros((nt, GUARD, 128), F32)

    view = ion.at[:, :, 8 : 8 + rows]
    pltpu.make_async_copy(view, view, sem_ion.at[0]).wait()
    step_i = 128 // (3 * n_rt)
    bands = [(s, c) for s in range(3) for c in range(n_rt)]
    pack(2, [ion[s, 0, 8 * c + 8 : 8 * c + 16, :] for s, c in bands], step_i, 0)
    pack(3, [ion[s, lt - 1, 8 * c + 8 : 8 * c + 16, :] for s, c in bands], step_i, 1)
    send_lon(2, rx_ion, 0, "ion")

    outer, inner = [0, PIECES - 1], list(range(1, PIECES - 1))
    slot_s = 4
    slot_v = slot_s + 2 * PIECES
    slot_in = slot_v + 2 * len(outer)
    slot_far = slot_in + 2 * len(inner)
    slot_fars = slot_far + 2 * len(inner)
    slot_corner = slot_fars + 2 * len(inner)

    def two_terms(own, other, rx, slot, far, recv):
        for i, q in enumerate(inner):
            home = [8 * (q * per + k) for k in range(per)]
            for side, t in enumerate((0, lt - 1)):
                a, b = slot + 2 * i + side, far + 2 * i + side
                pack(a, [own[t, r : r + 8, :] for r in home], EDGE, side * EDGE)
                pack(b, [other[t, r : r + 8, :] for r in home[::-1]], EDGE, side * EDGE)
                there = len(inner) - 1 - i
                rcopy(pk.at[a], rx.at[side, 0, i], (lf, rt)[side], "lon", recv).start()
                rcopy(pk.at[b], rx.at[side, 1, there], (far_lf, far_rt)[side], "lon", recv).start()

    from_dn("n_up", cur_n.at[:, 0:8])
    from_up("n_dn", cur_n.at[:, 0:8])
    arrived("e", rx_e)
    e_fr, e_fl = rx_e[0, 0, :, :], rx_e[1, 0, :, :]
    for q in [0, PIECES - 1] + list(range(1, PIECES - 1)):
        for c in range(q * per, (q + 1) * per):
            row = 8 * c
            at = slice(row, row + 8)
            left, right = shifts(
                [cur_e[t, at, :] for t in range(lt)],
                turn(e_fr, 127 - step_e * c), turn(e_fl, 128 - step_e * c),
            )
            for t in range(lt):
                d_lon = 0.5 * (right[t] - left[t])
                d_lat = 0.5 * (cur_n[t, row + 9 : row + 17, :] - cur_n[t, row + 7 : row + 15, :])
                s_one[t, at, :] = d_lon + d_lat
                t_out[t, at, :] = d_lon - d_lat
        if q in outer:
            send_t(q, "t_a")
        if q == outer[-1]:
            for b in inner:
                send_sig(b, "sig_b")
            two_terms(sig, sig, rx_ins, slot_s + 2 * len(outer), slot_fars, "inner_s")

    two_terms(s_one, t_out, rx_in, slot_in, slot_far, "inner")

    for j in range(nt):
        @pl.loop(0, 8, unroll=2)
        def _(c):
            row = lax.broadcasted_iota(jnp.int32, (16, 128), 0) + 16 * c
            col = lax.broadcasted_iota(jnp.int32, (16, 128), 1)
            home = row * nt + j
            for t in range(lt):
                here = col + t * 128
                back = jnp.where(home == here, 1.0, 0.0).astype(BF16)
                before = jnp.where(here == 0, width - 1, here - 1)
                slope = jnp.where(
                    home == here + 1, 0.5, jnp.where(home == before, -0.5, 0.0)
                ).astype(BF16)
                for part in range(3):
                    at = pl.ds(pl.multiple_of(part * width + j * 128 + 16 * c, 16), 16)
                    to_plain[at, t * 128 : (t + 1) * 128] = back
                    to_plain[at, (lt + t) * 128 : (lt + t + 1) * 128] = slope

    def combine(own, rx, out, q):
        p = PIECES - 1 - q
        for c in range(p * per, (p + 1) * per):
            back = rows - 8 - 8 * c
            for t in range(lt):
                out[t, 8 * c + GUARD : 8 * c + GUARD + 8, :] = own[
                    t, 8 * c : 8 * c + 8, :
                ] + rev8(rx[t, back : back + 8, :])

    def spread(out, rx, slot, g, lo, count, recv):
        tiles = lambda t: [out[t, lo + 8 * k : lo + 8 * k + 8, :] for k in range(count)]
        pack(slot, tiles(0), EDGE, 0)
        pack(slot + 1, tiles(lt - 1), EDGE, EDGE)
        send_lon(slot, rx, g, recv)

    def gather(out, rx, g, lo, count):
        fr, fl = rx[0, g, :, :], rx[1, g, :, :]
        for k in range(count):
            a, b = turn(fr, 128 - EDGE * k), turn(fl, 256 - EDGE - EDGE * k)
            out[lt, lo + 8 * k : lo + 8 * k + 8, :] = jnp.where(
                lane < EDGE, a, jnp.where(lane >= 128 - EDGE, b, 0.0)
            )

    def spread_piece(out, rx, slot, q, recv):
        p = PIECES - 1 - q
        spread(out, rx, slot, p, GUARD + p * per * 8, per, recv)

    def gather_piece(out, rx, q):
        p = PIECES - 1 - q
        gather(out, rx, p, GUARD + p * per * 8, per)

    def lat_send(out, rx, depth, name, slot):
        lo, hi = GUARD, GUARD + rows
        to_up(out.at[0:lt, lo : lo + depth], out.at[0:lt, hi : hi + depth], name + "_up")
        to_dn(out.at[0:lt, hi - depth : hi], out.at[0:lt, lo - depth : lo], name + "_dn")
        for edge, first in enumerate((lo, hi - depth)):
            for side, t in enumerate((0, lt - 1)):
                tiles = [out[t, r : r + 8, :] for r in range(first, first + depth, 8)]
                pack(slot + 2 * edge + side, tiles, EDGE, side * EDGE)

        def corners(edge, lat, send, recv):
            for side, lon in enumerate((lf[1], rt[1])):
                rcopy(
                    pk.at[slot + 2 * edge + side], rx.at[side, PIECES + 1 - edge], (lat, lon),
                    send, recv,
                ).start()

        @pl.when(has_up)
        def _():
            corners(0, up[0], "up_lon", name + "_hi")

        @pl.when(has_dn)
        def _():
            corners(1, dn[0], "dn_lon", name + "_lo")

    def lat_gather(out, rx, depth, name):
        lo, hi = GUARD, GUARD + rows

        @pl.when(has_up)
        def _():
            arrived(name + "_dn", out.at[0:lt, lo - depth : lo])
            arrived(name + "_lo", pk.at[0:2])
            gather(out, rx, PIECES, lo - depth, depth // 8)

        @pl.when(has_dn)
        def _():
            arrived(name + "_up", out.at[0:lt, lo - depth : lo])
            arrived(name + "_hi", pk.at[0:2])
            gather(out, rx, PIECES + 1, hi, depth // 8)

    arrived("ion", rx_ion)
    i_fr, i_fl = rx_ion[0, 0, :, :], rx_ion[1, 0, :, :]
    for k, (s, c) in enumerate(bands):
        at = slice(8 * c, 8 * c + 8)
        tiles = [ion[s, t, 8 * c + 8 : 8 * c + 16, :] for t in range(lt)]
        left, right = shifts(tiles, turn(i_fr, 127 - step_i * k), turn(i_fl, 128 - step_i * k))
        for t in range(lt):
            ion_a[s, t, at, :] = tiles[t] - left[t]
            ion_b[s, t, at, :] = right[t] - tiles[t]

    arrived("sig_a", sig_rx.at[:, 0 : 2 * per * 8])
    for q in outer:
        combine(sig, sig_rx, S, q)
    lat_send(S, rx_s, GUARD, "s", slot_corner)
    for i, q in enumerate(outer):
        spread_piece(S, rx_s, slot_s + 2 * i, q, "s_lon")

    arrived("t_a", t_rx.at[:, 0 : 2 * per * 8])
    for q in outer:
        combine(s_one, t_rx, src, q)
    lat_send(src, rx_v, HALO, "v", slot_corner + 4)
    for q in inner[:-1]:
        send_t(q, "t_b")
    send_t(inner[-1], "t_c")
    to_up(ion.at[:, :, 8:16], ion.at[:, :, rows + 8 : rows + 16], "i_up")
    to_dn(ion.at[:, :, rows : rows + 8], ion.at[:, :, 0:8], "i_dn")
    for i, q in enumerate(outer):
        spread_piece(src, rx_v, slot_v + 2 * i, q, "v_lon")

    def inner_edges(out, rx, pair, q):
        p = PIECES - 1 - q
        for side in range(2):
            rx[side, p, :, :] = pair[side, 0, p - 1, :, :] + rev8(pair[side, 1, p - 1, :, :])
        gather_piece(out, rx, q)

    arrived("sig_b", sig_rx.at[:, 0 : (PIECES - 2) * per * 8])
    for q in inner:
        combine(sig, sig_rx, S, q)
    arrived("inner_s", rx_ins)
    for q in inner:
        inner_edges(S, rx_s, rx_ins, q)
    arrived("s_lon", pk.at[0 : 2 * len(outer)])
    for q in outer:
        gather_piece(S, rx_s, q)
    lat_gather(S, rx_s, GUARD, "s")

    def split(v, at, t):
        for part in range(3):
            low = v.astype(BF16)
            lhs[at, part * width + t * 128 : part * width + (t + 1) * 128] = low
            v = v - low.astype(F32)

    def split_rows(ref, first, lo, hi):
        for row in range(lo, hi, 16):
            for t in range(nt):
                split(ref[t, row + first : row + first + 16, :], slice(row, row + 16), t)

    def conv_lon(v):
        after = v[1:] + [pltpu.roll(v[0], 127, 1)]
        p = [a + b for a, b in zip(v, after)]
        before = [pltpu.roll(p[-1], 1, 1)] + p[:-1]
        return [a + b for a, b in zip(p, before)]

    tall = rows + 2 * GUARD
    ext = rows + 2 * HALO
    split_rows(S, 0, 0, tall)
    moved = jnp.dot(lhs[0:tall, :], to_strided[...], preferred_element_type=F32)
    for t in range(nt):
        SP[t, :, :] = moved[:, t * 128 : (t + 1) * 128]

    for c in range(tall // 8):
        for t, v in enumerate(conv_lon([SP[t, 8 * c : 8 * c + 8, :] for t in range(nt)])):
            U[t, 8 * c : 8 * c + 8, :] = v

    total = rows * nlat
    skip = GUARD - HALO
    for c in range(R):
        where = sub * R + (c - HALO + me_lat * rows)
        inside = (where >= 0) & (where < total)
        at = slice(8 * c, 8 * c + 8)
        for t in range(nt):
            s = SP[t, pl.ds(skip + c, 8, stride=R), :]
            around = U[t, pl.ds(skip + c - 1, 8, stride=R), :] + U[
                t, pl.ds(skip + c + 1, 8, stride=R), :
            ]
            around = around + 2.0 * U[t, pl.ds(skip + c, 8, stride=R), :]
            inv = jnp.where(inside, 1.0 / (DAMPING + 2.0 * s + 0.25 * around), 0.0)
            quarter = 0.25 * inv
            SR[t, at, :] = s
            invR[t, at, :] = inv
            rR[t, at, :] = quarter
            mR[t, at, :] = (THETA - 1.0) - 8.0 * (quarter * s)
            X[1, t, at, :] = jnp.zeros((8, 128), F32)

    arrived("t_b", t_rx.at[:, 0 : (PIECES - 3) * per * 8])
    for q in inner[:-1]:
        combine(s_one, t_rx, src, q)
    arrived("inner", rx_in)
    for q in inner:
        inner_edges(src, rx_v, rx_in, q)
    arrived("v_lon", pk.at[0 : 2 * len(outer)])
    for q in outer:
        gather_piece(src, rx_v, q)
    lat_gather(src, rx_v, HALO, "v")
    last = PIECES - 1 - inner[-1]
    last_lo, last_hi = HALO + last * per * 8, HALO + (last + 1) * per * 8
    for lo, hi in ((0, last_lo), (last_hi, ext)):
        split_rows(src, skip, lo, hi)
        moved = jnp.dot(lhs[lo:hi, :], to_strided[...], preferred_element_type=F32)
        for t in range(nt):
            SP[t, lo:hi, :] = moved[:, t * 128 : (t + 1) * 128]

    arrived("t_c", t_rx.at[:, 0 : per * 8])
    combine(s_one, t_rx, src, inner[-1])
    split_rows(src, skip, last_lo, last_hi)
    moved = jnp.dot(lhs[last_lo:last_hi, :], to_strided[...], preferred_element_type=F32)
    for t in range(nt):
        SP[t, last_lo:last_hi, :] = moved[:, t * 128 : (t + 1) * 128]
    for c in range(R):
        at = slice(8 * c, 8 * c + 8)
        for t in range(nt):
            first = SP[t, pl.ds(c, 8, stride=R), :] * invR[t, at, :]
            spR[t, at, :] = first
            X[0, t, at, :] = first * (1.0 / THETA)

    def sweep(k, cur, prv, final):
        c1 = coef[0, k]
        c2 = coef[1, k]

        def smooth(c):
            at = slice(8 * c, 8 * c + 8)
            xs = [X[cur, t, at, :] for t in range(nt)]
            ys = [SR[t, at, :] * xs[t] for t in range(nt)]
            return xs, conv_lon(xs), conv_lon(ys)

        _, u_end, w_end = smooth(R - 1)
        xs, u, w = smooth(0)
        u_top, w_top = u, w
        qu = [pltpu.roll(a, 1, 0) + b for a, b in zip(u_end, u)]
        qw = [pltpu.roll(a, 1, 0) + b for a, b in zip(w_end, w)]
        for c in range(R):
            if c < R - 1:
                x_next, u_next, w_next = smooth(c + 1)
            else:
                x_next = None
                u_next = [pltpu.roll(v, 7, 0) for v in u_top]
                w_next = [pltpu.roll(v, 7, 0) for v in w_top]
            qu2 = [a + b for a, b in zip(u, u_next)]
            qw2 = [a + b for a, b in zip(w, w_next)]
            at = slice(8 * c, 8 * c + 8)
            for t in range(nt):
                pull = SR[t, at, :] * (qu[t] + qu2[t]) + (qw[t] + qw2[t])
                z = rR[t, at, :] * pull + (mR[t, at, :] * xs[t] + spR[t, at, :])
                new = c2 * z - c1 * X[prv, t, at, :]
                if final:
                    xr[t, pl.ds(8 + c, 8, stride=R), :] = new
                else:
                    X[prv, t, at, :] = new
            qu, qw, u, w, xs = qu2, qw2, u_next, w_next, x_next

    @pl.loop(0, (SWEEPS - 2) // 2)
    def _(k):
        sweep(2 * k, 0, 1, False)
        sweep(2 * k + 1, 1, 0, False)

    sweep(SWEEPS - 2, 0, 1, True)

    own0 = 8 + HALO
    best = jnp.zeros((8, 128), F32)
    for c in range(n_rt):
        lo = own0 + 8 * c
        x = [xr[t, lo : lo + 8, :] for t in range(nt)]
        after = x[1:] + [pltpu.roll(x[0], 127, 1)]
        before = [pltpu.roll(x[-1], 1, 1)] + x[:-1]
        for t in range(nt):
            speed = jnp.abs(0.5 * (xr[t, lo + 1 : lo + 9, :] - xr[t, lo - 1 : lo + 7, :]))
            speed = speed + jnp.abs(0.5 * (after[t] - before[t]))
            best = jnp.maximum(best, jnp.where(lane * nt + t < lt * 128, speed, 0.0))
    mx[0:1, :] = jnp.max(best, axis=0, keepdims=True)

    for o, dev in enumerate(others):
        rcopy(mx.at[0:1], mrx.at[o : o + 1], dev, "max", "max").start()

    near = rows + 16
    split_rows(xr, own0 - 8, 0, near)
    moved = jnp.dot(lhs[0:near, :], to_plain[...], preferred_element_type=F32)
    for t in range(lt):
        xn[t, :, :] = moved[:, t * 128 : (t + 1) * 128]
        dnb[t, :, :] = moved[:, (lt + t) * 128 : (lt + t + 1) * 128]
        pot_o[:, t * 128 : (t + 1) * 128] = moved[8 : 8 + rows, t * 128 : (t + 1) * 128]

    from_dn("i_up", ion.at[:, :, 0:8])
    from_up("i_dn", ion.at[:, :, 0:8])

    @pl.loop(0, n_rt, unroll=2)
    def _(c):
        row = pl.multiple_of(8 * c, 8)
        at = pl.ds(row, 8)
        for t in range(lt):
            de = -0.5 * (xn[t, pl.ds(row + 9, 8), :] - xn[t, pl.ds(row + 7, 8), :])
            dv = dnb[t, pl.ds(row + 8, 8), :]
            e_pos, e_neg = jnp.maximum(de, 0.0), jnp.minimum(de, 0.0)
            n_pos, n_neg = jnp.maximum(dv, 0.0), jnp.minimum(dv, 0.0)
            for s in range(3):
                n = ion[s, t, pl.ds(row + 8, 8), :]
                f = e_pos * ion_a[s, t, at, :] + e_neg * ion_b[s, t, at, :]
                f = f + n_pos * (n - ion[s, t, pl.ds(row + 7, 8), :])
                f = f + n_neg * (ion[s, t, pl.ds(row + 9, 8), :] - n)
                flux[s, t, at, :] = f

    arrived("max", mrx.at[0 : n_dev - 1])
    best = jnp.maximum(
        jnp.max(mrx[0 : n_dev - 1, :], axis=0, keepdims=True), mx[0:1, :]
    )
    best = jnp.max(best, axis=1, keepdims=True)
    step = jnp.broadcast_to(COURANT / (best + 1e-6), (8, 128))

    for s in range(3):
        scale = MOBILITY[s] * step

        @pl.loop(0, n_rt, unroll=2)
        def _(c):
            row = pl.multiple_of(8 * c, 8)
            for t in range(lt):
                upd_o[s, pl.ds(row, 8), t * 128 : (t + 1) * 128] = (
                    ion[s, t, pl.ds(row + 8, 8), :] - scale * flux[s, t, pl.ds(row, 8), :]
                )

    to_side = sig.at[:, 0 : 8 + 24 + GUARD + HALO]

    @pl.when(has_up)
    def _():
        sent("up", to_side)
        sent("up_lon", pk.at[0:4])

    @pl.when(has_dn)
    def _():
        sent("dn", to_side)
        sent("dn_lon", pk.at[0:4])

    sent("sig", sig)
    sent("t", t_out)
    sent("lon", pk.at[0:slot_corner])
    sent("max", mrx.at[0 : n_dev - 1])


def write_out(pot_v, upd_v, pot_h, upd_h, sem):
    copies = [pltpu.make_async_copy(upd_v.at[s], upd_h.at[s], sem.at[s]) for s in range(3)]
    copies.append(pltpu.make_async_copy(pot_v, pot_h, sem.at[3]))
    for c in copies:
        c.start()
    for c in copies:
        c.wait()


def solution(mesh):
    nlat, nlon = mesh.shape["lat"], mesh.shape["lon"]

    def shards(pedersen, hall_conductivity, east_wind, north_wind, ion_density):
        lev, rows, cols = pedersen.shape
        lt = cols // 128
        nt = lt + 1
        width = nt * 128
        tall = rows + 2 * GUARD
        ext = rows + 2 * HALO
        groups = PIECES + 2
        vm = lambda *shape: pltpu.VMEM(shape, F32)
        half = lambda *shape: pltpu.VMEM(shape, BF16)
        dma = lambda *shape: pltpu.SemaphoreType.DMA(shape)
        hbm = pl.BlockSpec(memory_space=pltpu.HBM)
        vmem = pl.BlockSpec(memory_space=pltpu.VMEM)
        pot, upd = pl.pallas_call(
            functools.partial(kernel, nlat, nlon, lev, rows, lt),
            out_shape=(pltpu.VMEM((rows, cols), F32), pltpu.VMEM((3, rows, cols), F32)),
            in_specs=[hbm] * 5,
            out_specs=(vmem, vmem),
            scratch_shapes=[vm(4, lev, rows, cols)]
            + [vm(3, lt, rows + 16, 128)] + [vm(3, lt, rows, 128)] * 2
            + [vm(lt, rows, 128), vm(lt, rows, 128), vm(lt, rows + 16, 128)]
            + [vm(lt, rows, 128)] * 4
            + [vm(nt, tall, 128)] * 2
            + [vm(10 * PIECES - 4, 8, 128)] + [vm(2, 1, 8, 128)] * 2 + [vm(2, groups, 8, 128)] * 2
            + [vm(2, 2, PIECES - 2, 8, 128)] * 2
            + [half(tall, 3 * width), half(3 * width, width), half(3 * width, 2 * lt * 128)]
            + [pltpu.SMEM((2, SWEEPS), F32)]
            + [vm(nt, tall, 128)] * 2
            + [vm(nt, ext, 128)] * 5
            + [vm(2, nt, ext, 128), vm(nt, ext + 16, 128)]
            + [vm(lt, rows + 16, 128)] * 2
            + [vm(3, lt, rows, 128), vm(8, 128), vm(nlat * nlon, 128)]
            + [dma(len(in_groups(rows // 8))), dma(1), dma(len(SEND)), dma(len(RECV))],
            compiler_params=pltpu.CompilerParams(
                collective_id=0, has_side_effects=True, vmem_limit_bytes=60 * 1024 * 1024
            ),
        )(pedersen, hall_conductivity, east_wind, north_wind, ion_density)
        pot = pltpu.with_memory_space_constraint(pot, pltpu.VMEM)
        upd = pltpu.with_memory_space_constraint(upd, pltpu.VMEM)
        return pl.pallas_call(
            write_out,
            out_shape=(
                jax.ShapeDtypeStruct((rows, cols), F32),
                jax.ShapeDtypeStruct((3, rows, cols), F32),
            ),
            in_specs=[vmem, vmem],
            out_specs=(hbm, hbm),
            scratch_shapes=[dma(4)],
        )(pot, upd)

    spec = P(None, "lat", "lon")
    return jax.shard_map(
        shards,
        mesh=mesh,
        in_specs=(spec,) * 5,
        out_specs=(P("lat", "lon"), spec),
        check_vma=False,
    )
```

```python
import functools

import jax
import jax.numpy as jnp
from jax import lax
from jax.experimental import pallas as pl
from jax.experimental.pallas import tpu as pltpu
from jax.sharding import PartitionSpec as P

SWEEPS = 16
DAMPING = 0.0001
LOW_BOUND = 0.05
HIGH_BOUND = 2.0
COURANT = 0.8
MOBILITY = (1.0, 0.6, 0.3)
MESH = pl.DeviceIdType.MESH
GUARD = 24
HALO = 16
PIECES = 4
THETA = 0.5 * (HIGH_BOUND + LOW_BOUND)
F32 = jnp.float32
BF16 = jnp.bfloat16


def chebyshev_factors():
    delta = 0.5 * (HIGH_BOUND - LOW_BOUND)
    sigma_one = THETA / delta
    rho_prev = 1.0 / sigma_one
    first_list = []
    second_list = []
    for sweep in range(SWEEPS):
        rho_next = 1.0 / (2.0 * sigma_one - rho_prev)
        first_list.append(rho_next * rho_prev)
        second_list.append(2.0 * rho_next / delta)
        rho_prev = rho_next
    return first_list, second_list


RECV = ("e", "ion", "n_up", "n_dn", "i_up", "i_dn", "sig_a", "sig_b", "t_a", "t_b",
        "s_up", "s_dn", "s_lo", "s_hi", "s_lon", "v_up", "v_dn", "v_lo", "v_hi", "v_lon",
        "inner", "inner_s", "max")
SEND = ("sig", "t", "lon", "up", "dn", "up_lon", "dn_lon", "max")
EDGE = 32


def in_groups(n_rt):
    per = n_rt // PIECES
    spans = [(0, 1), (n_rt - 1, n_rt), (1, per), (n_rt - per, n_rt - 1)]
    for q in range(1, PIECES - 1):
        half = q * per + per // 2
        spans += [(q * per, half), (half, (q + 1) * per)]
    return [p for p in spans if p[1] > p[0]]


def kernel(
    nlat, nlon, lev, rows, lt,
    ped_h, hall_h, east_h, north_h, ion_h,
    pot_o, upd_o,
    vin, ion, ion_a, ion_b,
    sig, cur_e, cur_n, s_one, t_out, sig_rx, t_rx,
    S, src, pk, rx_e, rx_ion, rx_s, rx_v, rx_in, rx_ins,
    lhs, to_strided, to_plain, coef,
    SP, U, SR, rR, mR, invR, spR, X, xr, xn, dnb,
    flux, mx, mrx,
    sem_in, sem_ion, ss, rs,
):
    n_rt = rows // 8
    nt = lt + 1
    width = nt * 128
    R = (rows + 2 * HALO) // 8
    n_dev = nlat * nlon
    me_lat = lax.axis_index("lat")
    me_lon = lax.axis_index("lon")
    has_up = me_lat > 0
    has_dn = me_lat < nlat - 1
    up = (jnp.maximum(me_lat - 1, 0), me_lon)
    dn = (jnp.minimum(me_lat + 1, nlat - 1), me_lon)
    lf = (me_lat, lax.rem(me_lon + nlon - 1, nlon))
    rt = (me_lat, lax.rem(me_lon + 1, nlon))
    mirror = (nlat - 1 - me_lat, me_lon)
    far_lf, far_rt = (mirror[0], lf[1]), (mirror[0], rt[1])
    others = [
        (lax.rem(me_lat + a, nlat), lax.rem(me_lon + b, nlon))
        for a in range(nlat) for b in range(nlon) if a or b
    ]

    barrier = pltpu.get_barrier_semaphore()
    for dev in others:
        pl.semaphore_signal(barrier, inc=1, device_id=dev, device_id_type=MESH)

    per = n_rt // PIECES
    groups = in_groups(n_rt)

    def in_copy(a, g):
        at = slice(8 * groups[g][0], 8 * groups[g][1])
        return pltpu.make_async_copy(
            (ped_h, hall_h, east_h, north_h)[a].at[:, at, :], vin.at[a, :, at, :], sem_in.at[g]
        )

    for g in range(len(groups)):
        for a in range(4):
            in_copy(a, g).start()
    for s in range(3):
        for t in range(lt):
            pltpu.make_async_copy(
                ion_h.at[s, :, t * 128 : (t + 1) * 128], ion.at[s, t, 8 : 8 + rows], sem_ion.at[0]
            ).start()

    first_list, second_list = chebyshev_factors()
    for k in range(SWEEPS):
        coef[0, k] = jnp.float32(first_list[k])
        coef[1, k] = jnp.float32(second_list[k])

    def rcopy(src_ref, dst_ref, dev, send, recv):
        return pltpu.make_async_remote_copy(
            src_ref=src_ref, dst_ref=dst_ref,
            send_sem=ss.at[SEND.index(send)], recv_sem=rs.at[RECV.index(recv)],
            device_id=dev, device_id_type=MESH,
        )

    def arrived(name, view):
        pltpu.make_async_copy(view, view, rs.at[RECV.index(name)]).wait()

    def sent(name, view):
        pltpu.make_async_copy(view, view, ss.at[SEND.index(name)]).wait()

    lane = lax.broadcasted_iota(jnp.int32, (8, 128), 1)
    sub = lax.broadcasted_iota(jnp.int32, (8, 128), 0)

    def turn(v, by):
        by = by % 128
        return pltpu.roll(v, by, 1) if by else v

    def shifts(v, after, before):
        a = [pltpu.roll(t, 1, 1) for t in v]
        b = [pltpu.roll(t, 127, 1) for t in v] + [after]
        left = [jnp.where(lane == 0, p, q) for p, q in zip([before] + a[:-1], a)]
        right = [jnp.where(lane == 127, p, q) for p, q in zip(b[1:], b[:-1])]
        return left, right

    def pack(slot, tiles, step, skip):
        acc = None
        for k, v in enumerate(tiles):
            v = turn(v, step * k + skip)
            acc = v if k == 0 else jnp.where(lane < step * k, acc, v)
        pk[slot, :, :] = acc

    def rev8(v):
        v = pltpu.roll(v, 4, 0)
        for b in (2, 1):
            v = jnp.where((sub & b) == 0, pltpu.roll(v, 8 - b, 0), pltpu.roll(v, b, 0))
        return v

    @pl.loop(0, width // 16, unroll=4)
    def _(c):
        row = lax.broadcasted_iota(jnp.int32, (16, 128), 0) + 16 * c
        col = lax.broadcasted_iota(jnp.int32, (16, 128), 1)
        for t in range(nt):
            there = jnp.where(row == col * nt + t, 1.0, 0.0).astype(BF16)
            for part in range(3):
                at = pl.ds(pl.multiple_of(part * width + 16 * c, 16), 16)
                to_strided[at, t * 128 : (t + 1) * 128] = there

    weight = [(0.5 + l / lev) / lev for l in range(lev)]

    def columns(g):
        lo, hi = groups[g]
        view = vin.at[:, :, 8 * lo : 8 * hi, :]
        pltpu.make_async_copy(view, view, sem_in.at[g]).wait()

        @pl.loop(lo, hi)
        def _(c):
            row = pl.multiple_of(8 * c, 8)
            for t in range(lt):
                at = (pl.ds(row, 8), slice(t * 128, (t + 1) * 128))
                acc = [jnp.zeros((8, 128), F32)] * 3
                for l in range(lev):
                    p, h = weight[l] * vin[(0, l) + at], weight[l] * vin[(1, l) + at]
                    e, n = vin[(2, l) + at], vin[(3, l) + at]
                    acc = [acc[0] + p, acc[1] + (p * e + h * n), acc[2] + (p * n - h * e)]
                sig[t, pl.ds(row, 8), :] = acc[0]
                cur_e[t, pl.ds(row, 8), :] = acc[1]
                cur_n[t, pl.ds(row + 8, 8), :] = acc[2]

    def band(q):
        return slice(q * per * 8, (q + 1) * per * 8)

    def send_sig(q, recv):
        rcopy(sig.at[:, band(q)], sig_rx.at[:, band(q)], mirror, "sig", recv).start()

    def send_t(q, recv):
        rcopy(t_out.at[:, band(q)], t_rx.at[:, band(q)], mirror, "t", recv).start()

    def to_up(src_ref, dst_ref, recv):
        @pl.when(has_up)
        def _():
            rcopy(src_ref, dst_ref, up, "up", recv).start()

    def to_dn(src_ref, dst_ref, recv):
        @pl.when(has_dn)
        def _():
            rcopy(src_ref, dst_ref, dn, "dn", recv).start()

    def from_dn(name, view):
        @pl.when(has_dn)
        def _():
            arrived(name, view)

    def from_up(name, view):
        @pl.when(has_up)
        def _():
            arrived(name, view)

    def send_lon(slot, rx, g, recv):
        rcopy(pk.at[slot], rx.at[0, g], lf, "lon", recv).start()
        rcopy(pk.at[slot + 1], rx.at[1, g], rt, "lon", recv).start()

    columns(0)
    columns(1)
    pl.semaphore_wait(barrier, n_dev - 1)
    to_up(cur_n.at[:, 8:9], cur_n.at[:, rows + 8 : rows + 9], "n_up")
    to_dn(cur_n.at[:, rows + 7 : rows + 8], cur_n.at[:, 7:8], "n_dn")
    columns(2)
    send_sig(0, "sig_a")
    columns(3)
    send_sig(PIECES - 1, "sig_a")
    for q in range(1, PIECES - 1):
        columns(2 * q + 2)
        columns(2 * q + 3)
        if q != PIECES - 2:
            send_sig(q, "sig_b")

    step_e = 128 // n_rt
    pack(0, [cur_e[0, 8 * c : 8 * c + 8, :] for c in range(n_rt)], step_e, 0)
    pack(1, [cur_e[lt - 1, 8 * c : 8 * c + 8, :] for c in range(n_rt)], step_e, 1)
    send_lon(0, rx_e, 0, "e")

    outer, inner = [0, PIECES - 1], list(range(1, PIECES - 1))
    slot_s = 4
    slot_fars = slot_s + 2 * PIECES
    slot_v = slot_fars + 2 * len(inner)
    slot_in = slot_v + 2 * len(outer)
    slot_far = slot_in + 2
    slot_corner = slot_far + 2

    def two_terms(own, other, rx, slot, far, runs, edge, recv):
        for i, (lo, hi) in enumerate(runs):
            there = runs.index((n_rt - hi, n_rt - lo))
            for side, t in enumerate((0, lt - 1)):
                a, b = slot + 2 * i + side, far + 2 * i + side
                pack(a, [own[t, 8 * k : 8 * k + 8, :] for k in range(lo, hi)], edge, side * edge)
                pack(
                    b, [other[t, 8 * k : 8 * k + 8, :] for k in range(lo, hi)][::-1],
                    edge, side * edge,
                )
                rcopy(pk.at[a], rx.at[side, 0, i], (lf, rt)[side], "lon", recv).start()
                rcopy(pk.at[b], rx.at[side, 1, there], (far_lf, far_rt)[side], "lon", recv).start()

    two_terms(
        sig, sig, rx_ins, slot_s + 2 * len(outer), slot_fars,
        [(q * per, (q + 1) * per) for q in inner], EDGE, "inner_s",
    )

    @pl.when(jnp.logical_not(has_up))
    def _():
        cur_n[:, 0:8, :] = jnp.zeros((lt, 8, 128), F32)
        ion[:, :, 0:8, :] = jnp.zeros((3, lt, 8, 128), F32)
        S[:, 0:GUARD, :] = jnp.zeros((nt, GUARD, 128), F32)
        src[:, 0:GUARD, :] = jnp.zeros((nt, GUARD, 128), F32)

    @pl.when(jnp.logical_not(has_dn))
    def _():
        cur_n[:, rows + 8 : rows + 16, :] = jnp.zeros((lt, 8, 128), F32)
        ion[:, :, rows + 8 : rows + 16, :] = jnp.zeros((3, lt, 8, 128), F32)
        S[:, GUARD + rows :, :] = jnp.zeros((nt, GUARD, 128), F32)
        src[:, GUARD + rows :, :] = jnp.zeros((nt, GUARD, 128), F32)

    view = ion.at[:, :, 8 : 8 + rows]
    pltpu.make_async_copy(view, view, sem_ion.at[0]).wait()
    step_i = 128 // (3 * n_rt)
    bands = [(s, c) for s in range(3) for c in range(n_rt)]
    pack(2, [ion[s, 0, 8 * c + 8 : 8 * c + 16, :] for s, c in bands], step_i, 0)
    pack(3, [ion[s, lt - 1, 8 * c + 8 : 8 * c + 16, :] for s, c in bands], step_i, 1)
    send_lon(2, rx_ion, 0, "ion")

    from_dn("n_up", cur_n.at[:, 7:8])
    from_up("n_dn", cur_n.at[:, 7:8])
    arrived("e", rx_e)
    e_fr, e_fl = rx_e[0, 0, :, :], rx_e[1, 0, :, :]
    for q in [0, PIECES - 1] + list(range(1, PIECES - 1)):
        for c in range(q * per, (q + 1) * per):
            row = 8 * c
            at = slice(row, row + 8)
            left, right = shifts(
                [cur_e[t, at, :] for t in range(lt)],
                turn(e_fr, 127 - step_e * c), turn(e_fl, 128 - step_e * c),
            )
            for t in range(lt):
                d_lon = 0.5 * (right[t] - left[t])
                d_lat = 0.5 * (cur_n[t, row + 9 : row + 17, :] - cur_n[t, row + 7 : row + 15, :])
                s_one[t, at, :] = d_lon + d_lat
                t_out[t, at, :] = d_lon - d_lat
        if q in outer:
            send_t(q, "t_a")
    send_sig(PIECES - 2, "sig_b")
    mid = (per, n_rt - per)
    edge_in = 128 // (mid[1] - mid[0])
    two_terms(s_one, t_out, rx_in, slot_in, slot_far, [mid], edge_in, "inner")

    for j in range(nt):
        @pl.loop(0, 8, unroll=2)
        def _(c):
            row = lax.broadcasted_iota(jnp.int32, (16, 128), 0) + 16 * c
            col = lax.broadcasted_iota(jnp.int32, (16, 128), 1)
            home = row * nt + j
            for t in range(lt):
                here = col + t * 128
                back = jnp.where(home == here, 1.0, 0.0).astype(BF16)
                before = jnp.where(here == 0, width - 1, here - 1)
                slope = jnp.where(
                    home == here + 1, 0.5, jnp.where(home == before, -0.5, 0.0)
                ).astype(BF16)
                for part in range(3):
                    at = pl.ds(pl.multiple_of(part * width + j * 128 + 16 * c, 16), 16)
                    to_plain[at, t * 128 : (t + 1) * 128] = back
                    to_plain[at, (lt + t) * 128 : (lt + t + 1) * 128] = slope

    def combine(own, rx, out, q):
        p = PIECES - 1 - q
        for c in range(p * per, (p + 1) * per):
            back = rows - 8 - 8 * c
            for t in range(lt):
                out[t, 8 * c + GUARD : 8 * c + GUARD + 8, :] = own[
                    t, 8 * c : 8 * c + 8, :
                ] + rev8(rx[t, back : back + 8, :])

    def spread(out, rx, slot, g, lo, count, recv):
        tiles = lambda t: [out[t, lo + 8 * k : lo + 8 * k + 8, :] for k in range(count)]
        pack(slot, tiles(0), EDGE, 0)
        pack(slot + 1, tiles(lt - 1), EDGE, EDGE)
        send_lon(slot, rx, g, recv)

    def unpack(out, fr, fl, lo, count, edge):
        for k in range(count):
            a, b = turn(fr, 128 - edge * k), turn(fl, 256 - edge - edge * k)
            out[lt, lo + 8 * k : lo + 8 * k + 8, :] = jnp.where(
                lane < edge, a, jnp.where(lane >= 128 - edge, b, 0.0)
            )

    def gather(out, rx, g, lo, count):
        unpack(out, rx[0, g, :, :], rx[1, g, :, :], lo, count, EDGE)

    def spread_piece(out, rx, slot, q, recv):
        p = PIECES - 1 - q
        spread(out, rx, slot, p, GUARD + p * per * 8, per, recv)

    def gather_piece(out, rx, q):
        p = PIECES - 1 - q
        gather(out, rx, p, GUARD + p * per * 8, per)

    def lat_send(out, rx, depth, name, slot):
        lo, hi = GUARD, GUARD + rows
        to_up(out.at[0:lt, lo : lo + depth], out.at[0:lt, hi : hi + depth], name + "_up")
        to_dn(out.at[0:lt, hi - depth : hi], out.at[0:lt, lo - depth : lo], name + "_dn")
        for edge, first in enumerate((lo, hi - depth)):
            for side, t in enumerate((0, lt - 1)):
                tiles = [out[t, r : r + 8, :] for r in range(first, first + depth, 8)]
                pack(slot + 2 * edge + side, tiles, EDGE, side * EDGE)

        def corners(edge, lat, send, recv):
            for side, lon in enumerate((lf[1], rt[1])):
                rcopy(
                    pk.at[slot + 2 * edge + side], rx.at[side, PIECES + 1 - edge], (lat, lon),
                    send, recv,
                ).start()

        @pl.when(has_up)
        def _():
            corners(0, up[0], "up_lon", name + "_hi")

        @pl.when(has_dn)
        def _():
            corners(1, dn[0], "dn_lon", name + "_lo")

    def lat_gather(out, rx, depth, name):
        lo, hi = GUARD, GUARD + rows

        @pl.when(has_up)
        def _():
            arrived(name + "_dn", out.at[0:lt, lo - depth : lo])
            arrived(name + "_lo", pk.at[0:2])
            gather(out, rx, PIECES, lo - depth, depth // 8)

        @pl.when(has_dn)
        def _():
            arrived(name + "_up", out.at[0:lt, lo - depth : lo])
            arrived(name + "_hi", pk.at[0:2])
            gather(out, rx, PIECES + 1, hi, depth // 8)

    arrived("ion", rx_ion)
    i_fr, i_fl = rx_ion[0, 0, :, :], rx_ion[1, 0, :, :]
    for k, (s, c) in enumerate(bands):
        at = slice(8 * c, 8 * c + 8)
        tiles = [ion[s, t, 8 * c + 8 : 8 * c + 16, :] for t in range(lt)]
        left, right = shifts(tiles, turn(i_fr, 127 - step_i * k), turn(i_fl, 128 - step_i * k))
        for t in range(lt):
            ion_a[s, t, at, :] = tiles[t] - left[t]
            ion_b[s, t, at, :] = right[t] - tiles[t]

    arrived("sig_a", sig_rx.at[:, 0 : 2 * per * 8])
    for q in outer:
        combine(sig, sig_rx, S, q)
    lat_send(S, rx_s, GUARD, "s", slot_corner)
    for i, q in enumerate(outer):
        spread_piece(S, rx_s, slot_s + 2 * i, q, "s_lon")

    arrived("t_a", t_rx.at[:, 0 : 2 * per * 8])
    for q in outer:
        combine(s_one, t_rx, src, q)
    lat_send(src, rx_v, HALO, "v", slot_corner + 4)
    for q in inner:
        send_t(q, "t_b")
    to_up(ion.at[:, :, 8:9], ion.at[:, :, rows + 8 : rows + 9], "i_up")
    to_dn(ion.at[:, :, rows + 7 : rows + 8], ion.at[:, :, 7:8], "i_dn")
    for i, q in enumerate(outer):
        spread_piece(src, rx_v, slot_v + 2 * i, q, "v_lon")

    def inner_edges(out, pair, i, lo, count, edge):
        fr, fl = [pair[side, 0, i, :, :] + rev8(pair[side, 1, i, :, :]) for side in range(2)]
        unpack(out, fr, fl, GUARD + 8 * lo, count, edge)

    arrived("sig_b", sig_rx.at[:, 0 : (PIECES - 2) * per * 8])
    for q in inner:
        combine(sig, sig_rx, S, q)
    arrived("inner_s", rx_ins)
    for i, q in enumerate(inner):
        inner_edges(S, rx_ins, i, q * per, per, EDGE)
    arrived("s_lon", pk.at[0 : 2 * len(outer)])
    for q in outer:
        gather_piece(S, rx_s, q)
    lat_gather(S, rx_s, GUARD, "s")

    def split(v, at, t):
        for part in range(3):
            low = v.astype(BF16)
            lhs[at, part * width + t * 128 : part * width + (t + 1) * 128] = low
            v = v - low.astype(F32)

    def split_rows(ref, first, lo, hi):
        for row in range(lo, hi, 16):
            for t in range(nt):
                split(ref[t, row + first : row + first + 16, :], slice(row, row + 16), t)

    def conv_lon(v):
        after = v[1:] + [pltpu.roll(v[0], 127, 1)]
        p = [a + b for a, b in zip(v, after)]
        before = [pltpu.roll(p[-1], 1, 1)] + p[:-1]
        return [a + b for a, b in zip(p, before)]

    tall = rows + 2 * GUARD
    ext = rows + 2 * HALO
    split_rows(S, 0, 0, tall)
    moved = jnp.dot(lhs[0:tall, :], to_strided[...], preferred_element_type=F32)
    for t in range(nt):
        SP[t, :, :] = moved[:, t * 128 : (t + 1) * 128]

    for c in range(tall // 8):
        for t, v in enumerate(conv_lon([SP[t, 8 * c : 8 * c + 8, :] for t in range(nt)])):
            U[t, 8 * c : 8 * c + 8, :] = v

    total = rows * nlat
    skip = GUARD - HALO
    for c in range(R):
        where = sub * R + (c - HALO + me_lat * rows)
        inside = (where >= 0) & (where < total)
        at = slice(8 * c, 8 * c + 8)
        for t in range(nt):
            s = SP[t, pl.ds(skip + c, 8, stride=R), :]
            around = U[t, pl.ds(skip + c - 1, 8, stride=R), :] + U[
                t, pl.ds(skip + c + 1, 8, stride=R), :
            ]
            around = around + 2.0 * U[t, pl.ds(skip + c, 8, stride=R), :]
            inv = jnp.where(inside, 1.0 / (DAMPING + 2.0 * s + 0.25 * around), 0.0)
            quarter = 0.25 * inv
            SR[t, at, :] = s
            invR[t, at, :] = inv
            rR[t, at, :] = quarter
            mR[t, at, :] = (THETA - 1.0) - 8.0 * (quarter * s)
            X[1, t, at, :] = jnp.zeros((8, 128), F32)

    def transform(lo, hi):
        split_rows(src, skip, lo, hi)
        moved = jnp.dot(lhs[lo:hi, :], to_strided[...], preferred_element_type=F32)
        for t in range(nt):
            SP[t, lo:hi, :] = moved[:, t * 128 : (t + 1) * 128]

    arrived("v_lon", pk.at[0 : 2 * len(outer)])
    for q in outer:
        gather_piece(src, rx_v, q)
    lat_gather(src, rx_v, HALO, "v")
    late_lo, late_hi = HALO + 8 * mid[0], HALO + 8 * mid[1]
    transform(0, late_lo)
    transform(late_hi, ext)
    arrived("inner", rx_in)
    inner_edges(src, rx_in, 0, mid[0], mid[1] - mid[0], edge_in)
    arrived("t_b", t_rx.at[:, 0 : 8 * (mid[1] - mid[0])])
    for q in inner:
        combine(s_one, t_rx, src, q)
    transform(late_lo, late_hi)
    for c in range(R):
        at = slice(8 * c, 8 * c + 8)
        for t in range(nt):
            first = SP[t, pl.ds(c, 8, stride=R), :] * invR[t, at, :]
            spR[t, at, :] = first
            X[0, t, at, :] = first * (1.0 / THETA)

    def sweep(k, cur, prv, final):
        c1 = coef[0, k]
        c2 = coef[1, k]

        def smooth(c):
            at = slice(8 * c, 8 * c + 8)
            xs = [X[cur, t, at, :] for t in range(nt)]
            ys = [SR[t, at, :] * xs[t] for t in range(nt)]
            return xs, conv_lon(xs), conv_lon(ys)

        _, u_end, w_end = smooth(R - 1)
        xs, u, w = smooth(0)
        u_top, w_top = u, w
        qu = [pltpu.roll(a, 1, 0) + b for a, b in zip(u_end, u)]
        qw = [pltpu.roll(a, 1, 0) + b for a, b in zip(w_end, w)]
        for c in range(R):
            if c < R - 1:
                x_next, u_next, w_next = smooth(c + 1)
            else:
                x_next = None
                u_next = [pltpu.roll(v, 7, 0) for v in u_top]
                w_next = [pltpu.roll(v, 7, 0) for v in w_top]
            qu2 = [a + b for a, b in zip(u, u_next)]
            qw2 = [a + b for a, b in zip(w, w_next)]
            at = slice(8 * c, 8 * c + 8)
            for t in range(nt):
                pull = SR[t, at, :] * (qu[t] + qu2[t]) + (qw[t] + qw2[t])
                z = rR[t, at, :] * pull + (mR[t, at, :] * xs[t] + spR[t, at, :])
                new = c2 * z - c1 * X[prv, t, at, :]
                if final:
                    xr[t, pl.ds(8 + c, 8, stride=R), :] = new
                else:
                    X[prv, t, at, :] = new
            qu, qw, u, w, xs = qu2, qw2, u_next, w_next, x_next

    @pl.loop(0, (SWEEPS - 2) // 2)
    def _(k):
        sweep(2 * k, 0, 1, False)
        sweep(2 * k + 1, 1, 0, False)

    sweep(SWEEPS - 2, 0, 1, True)

    own0 = 8 + HALO
    best = jnp.zeros((8, 128), F32)
    for c in range(n_rt):
        lo = own0 + 8 * c
        x = [xr[t, lo : lo + 8, :] for t in range(nt)]
        after = x[1:] + [pltpu.roll(x[0], 127, 1)]
        before = [pltpu.roll(x[-1], 1, 1)] + x[:-1]
        for t in range(nt):
            speed = jnp.abs(0.5 * (xr[t, lo + 1 : lo + 9, :] - xr[t, lo - 1 : lo + 7, :]))
            speed = speed + jnp.abs(0.5 * (after[t] - before[t]))
            best = jnp.maximum(best, jnp.where(lane * nt + t < lt * 128, speed, 0.0))
    mx[0:1, :] = jnp.max(best, axis=0, keepdims=True)

    for o, dev in enumerate(others):
        rcopy(mx.at[0:1], mrx.at[o : o + 1], dev, "max", "max").start()

    near = rows + 16
    split_rows(xr, own0 - 8, 0, near)
    moved = jnp.dot(lhs[0:near, :], to_plain[...], preferred_element_type=F32)
    for t in range(lt):
        xn[t, :, :] = moved[:, t * 128 : (t + 1) * 128]
        dnb[t, :, :] = moved[:, (lt + t) * 128 : (lt + t + 1) * 128]
        pot_o[:, t * 128 : (t + 1) * 128] = moved[8 : 8 + rows, t * 128 : (t + 1) * 128]

    from_dn("i_up", ion.at[:, :, 7:8])
    from_up("i_dn", ion.at[:, :, 7:8])

    @pl.loop(0, n_rt, unroll=2)
    def _(c):
        row = pl.multiple_of(8 * c, 8)
        at = pl.ds(row, 8)
        for t in range(lt):
            de = -0.5 * (xn[t, pl.ds(row + 9, 8), :] - xn[t, pl.ds(row + 7, 8), :])
            dv = dnb[t, pl.ds(row + 8, 8), :]
            e_pos, e_neg = jnp.maximum(de, 0.0), jnp.minimum(de, 0.0)
            n_pos, n_neg = jnp.maximum(dv, 0.0), jnp.minimum(dv, 0.0)
            for s in range(3):
                n = ion[s, t, pl.ds(row + 8, 8), :]
                f = e_pos * ion_a[s, t, at, :] + e_neg * ion_b[s, t, at, :]
                f = f + n_pos * (n - ion[s, t, pl.ds(row + 7, 8), :])
                f = f + n_neg * (ion[s, t, pl.ds(row + 9, 8), :] - n)
                flux[s, t, at, :] = f

    arrived("max", mrx.at[0 : n_dev - 1])
    best = jnp.maximum(
        jnp.max(mrx[0 : n_dev - 1, :], axis=0, keepdims=True), mx[0:1, :]
    )
    best = jnp.max(best, axis=1, keepdims=True)
    step = jnp.broadcast_to(COURANT / (best + 1e-6), (8, 128))

    for s in range(3):
        scale = MOBILITY[s] * step

        @pl.loop(0, n_rt, unroll=2)
        def _(c):
            row = pl.multiple_of(8 * c, 8)
            for t in range(lt):
                upd_o[s, pl.ds(row, 8), t * 128 : (t + 1) * 128] = (
                    ion[s, t, pl.ds(row + 8, 8), :] - scale * flux[s, t, pl.ds(row, 8), :]
                )

    to_side = sig.at[:, 0 : 1 + 3 + GUARD + HALO]

    @pl.when(has_up)
    def _():
        sent("up", to_side)
        sent("up_lon", pk.at[0:4])

    @pl.when(has_dn)
    def _():
        sent("dn", to_side)
        sent("dn_lon", pk.at[0:4])

    sent("sig", sig)
    sent("t", t_out)
    sent("lon", pk.at[0:slot_corner])
    sent("max", mrx.at[0 : n_dev - 1])


def write_out(pot_v, upd_v, pot_h, upd_h, sem):
    copies = [pltpu.make_async_copy(upd_v.at[s], upd_h.at[s], sem.at[s]) for s in range(3)]
    copies.append(pltpu.make_async_copy(pot_v, pot_h, sem.at[3]))
    for c in copies:
        c.start()
    for c in copies:
        c.wait()


def solution(mesh):
    nlat, nlon = mesh.shape["lat"], mesh.shape["lon"]

    def shards(pedersen, hall_conductivity, east_wind, north_wind, ion_density):
        lev, rows, cols = pedersen.shape
        lt = cols // 128
        nt = lt + 1
        width = nt * 128
        tall = rows + 2 * GUARD
        ext = rows + 2 * HALO
        groups = PIECES + 2
        vm = lambda *shape: pltpu.VMEM(shape, F32)
        half = lambda *shape: pltpu.VMEM(shape, BF16)
        dma = lambda *shape: pltpu.SemaphoreType.DMA(shape)
        hbm = pl.BlockSpec(memory_space=pltpu.HBM)
        vmem = pl.BlockSpec(memory_space=pltpu.VMEM)
        pot, upd = pl.pallas_call(
            functools.partial(kernel, nlat, nlon, lev, rows, lt),
            out_shape=(pltpu.VMEM((rows, cols), F32), pltpu.VMEM((3, rows, cols), F32)),
            in_specs=[hbm] * 5,
            out_specs=(vmem, vmem),
            scratch_shapes=[vm(4, lev, rows, cols)]
            + [vm(3, lt, rows + 16, 128)] + [vm(3, lt, rows, 128)] * 2
            + [vm(lt, rows, 128), vm(lt, rows, 128), vm(lt, rows + 16, 128)]
            + [vm(lt, rows, 128)] * 4
            + [vm(nt, tall, 128)] * 2
            + [vm(8 * PIECES, 8, 128)] + [vm(2, 1, 8, 128)] * 2 + [vm(2, groups, 8, 128)] * 2
            + [vm(2, 2, 1, 8, 128), vm(2, 2, PIECES - 2, 8, 128)]
            + [half(tall, 3 * width), half(3 * width, width), half(3 * width, 2 * lt * 128)]
            + [pltpu.SMEM((2, SWEEPS), F32)]
            + [vm(nt, tall, 128)] * 2
            + [vm(nt, ext, 128)] * 5
            + [vm(2, nt, ext, 128), vm(nt, ext + 16, 128)]
            + [vm(lt, rows + 16, 128)] * 2
            + [vm(3, lt, rows, 128), vm(8, 128), vm(nlat * nlon, 128)]
            + [dma(len(in_groups(rows // 8))), dma(1), dma(len(SEND)), dma(len(RECV))],
            compiler_params=pltpu.CompilerParams(
                collective_id=0, has_side_effects=True, vmem_limit_bytes=60 * 1024 * 1024
            ),
        )(pedersen, hall_conductivity, east_wind, north_wind, ion_density)
        pot = pltpu.with_memory_space_constraint(pot, pltpu.VMEM)
        upd = pltpu.with_memory_space_constraint(upd, pltpu.VMEM)
        return pl.pallas_call(
            write_out,
            out_shape=(
                jax.ShapeDtypeStruct((rows, cols), F32),
                jax.ShapeDtypeStruct((3, rows, cols), F32),
            ),
            in_specs=[vmem, vmem],
            out_specs=(hbm, hbm),
            scratch_shapes=[dma(4)],
        )(pot, upd)

    spec = P(None, "lat", "lon")
    return jax.shard_map(
        shards,
        mesh=mesh,
        in_specs=(spec,) * 5,
        out_specs=(P("lat", "lon"), spec),
        check_vma=False,
    )
```

```python
import functools

import jax
import jax.numpy as jnp
from jax import lax
from jax.experimental import pallas as pl
from jax.experimental.pallas import tpu as pltpu
from jax.sharding import PartitionSpec as P

SWEEPS = 16
DAMPING = 0.0001
LOW_BOUND = 0.05
HIGH_BOUND = 2.0
COURANT = 0.8
MOBILITY = (1.0, 0.6, 0.3)
MESH = pl.DeviceIdType.MESH
GUARD = 24
HALO = 16
PIECES = 4
THETA = 0.5 * (HIGH_BOUND + LOW_BOUND)
F32 = jnp.float32
BF16 = jnp.bfloat16


def chebyshev_factors():
    delta = 0.5 * (HIGH_BOUND - LOW_BOUND)
    sigma_one = THETA / delta
    rho_prev = 1.0 / sigma_one
    first_list = []
    second_list = []
    for sweep in range(SWEEPS):
        rho_next = 1.0 / (2.0 * sigma_one - rho_prev)
        first_list.append(rho_next * rho_prev)
        second_list.append(2.0 * rho_next / delta)
        rho_prev = rho_next
    return first_list, second_list


RECV = ("e", "ion", "n_up", "n_dn", "i_up", "i_dn", "sig_a", "sig_b", "t_a", "t_b",
        "s_up", "s_dn", "s_lo", "s_hi", "s_lon", "v_up", "v_dn", "v_lo", "v_hi", "v_lon",
        "inner", "inner_s", "max")
SEND = ("sig", "t", "lon", "up", "dn", "up_lon", "dn_lon", "max")
EDGE = 32


def in_groups(n_rt):
    per = n_rt // PIECES
    spans = [(0, 1), (n_rt - 1, n_rt), (1, per), (n_rt - per, n_rt - 1)]
    for q in range(1, PIECES - 1):
        half = q * per + per // 2
        spans += [(q * per, half), (half, (q + 1) * per)]
    return [p for p in spans if p[1] > p[0]]


def kernel(
    nlat, nlon, lev, rows, lt,
    ped_h, hall_h, east_h, north_h, ion_h,
    pot_o, upd_o,
    vin, ion, ion_a, ion_b,
    sig, cur_e, cur_n, s_one, t_out, sig_rx, t_rx,
    S, src, pk, rx_e, rx_ion, rx_s, rx_v, rx_in, rx_ins,
    lhs, to_strided, to_plain, coef,
    SP, U, SR, rR, mR, invR, spR, X, xr, xn, dnb,
    flux, mx, mrx,
    sem_in, sem_ion, ss, rs,
):
    n_rt = rows // 8
    nt = lt + 1
    width = nt * 128
    R = (rows + 2 * HALO) // 8
    n_dev = nlat * nlon
    me_lat = lax.axis_index("lat")
    me_lon = lax.axis_index("lon")
    has_up = me_lat > 0
    has_dn = me_lat < nlat - 1
    up = (jnp.maximum(me_lat - 1, 0), me_lon)
    dn = (jnp.minimum(me_lat + 1, nlat - 1), me_lon)
    lf = (me_lat, lax.rem(me_lon + nlon - 1, nlon))
    rt = (me_lat, lax.rem(me_lon + 1, nlon))
    mirror = (nlat - 1 - me_lat, me_lon)
    far_lf, far_rt = (mirror[0], lf[1]), (mirror[0], rt[1])
    others = [
        (lax.rem(me_lat + a, nlat), lax.rem(me_lon + b, nlon))
        for a in range(nlat) for b in range(nlon) if a or b
    ]

    barrier = pltpu.get_barrier_semaphore()
    for dev in others:
        pl.semaphore_signal(barrier, inc=1, device_id=dev, device_id_type=MESH)

    per = n_rt // PIECES
    groups = in_groups(n_rt)

    def in_copy(a, g):
        at = slice(8 * groups[g][0], 8 * groups[g][1])
        return pltpu.make_async_copy(
            (ped_h, hall_h, east_h, north_h)[a].at[:, at, :], vin.at[a, :, at, :], sem_in.at[g]
        )

    for g in range(len(groups)):
        for a in range(4):
            in_copy(a, g).start()
    for s in range(3):
        for t in range(lt):
            pltpu.make_async_copy(
                ion_h.at[s, :, t * 128 : (t + 1) * 128], ion.at[s, t, 8 : 8 + rows], sem_ion.at[0]
            ).start()

    first_list, second_list = chebyshev_factors()
    for k in range(SWEEPS):
        coef[0, k] = jnp.float32(first_list[k])
        coef[1, k] = jnp.float32(second_list[k])

    def rcopy(src_ref, dst_ref, dev, send, recv):
        return pltpu.make_async_remote_copy(
            src_ref=src_ref, dst_ref=dst_ref,
            send_sem=ss.at[SEND.index(send)], recv_sem=rs.at[RECV.index(recv)],
            device_id=dev, device_id_type=MESH,
        )

    def arrived(name, view):
        pltpu.make_async_copy(view, view, rs.at[RECV.index(name)]).wait()

    def sent(name, view):
        pltpu.make_async_copy(view, view, ss.at[SEND.index(name)]).wait()

    lane = lax.broadcasted_iota(jnp.int32, (8, 128), 1)
    sub = lax.broadcasted_iota(jnp.int32, (8, 128), 0)

    def turn(v, by):
        by = by % 128
        return pltpu.roll(v, by, 1) if by else v

    def shifts(v, after, before):
        a = [pltpu.roll(t, 1, 1) for t in v]
        b = [pltpu.roll(t, 127, 1) for t in v] + [after]
        left = [jnp.where(lane == 0, p, q) for p, q in zip([before] + a[:-1], a)]
        right = [jnp.where(lane == 127, p, q) for p, q in zip(b[1:], b[:-1])]
        return left, right

    def pack(slot, tiles, step, skip):
        acc = None
        for k, v in enumerate(tiles):
            v = turn(v, step * k + skip)
            acc = v if k == 0 else jnp.where(lane < step * k, acc, v)
        pk[slot, :, :] = acc

    def rev8(v):
        v = pltpu.roll(v, 4, 0)
        for b in (2, 1):
            v = jnp.where((sub & b) == 0, pltpu.roll(v, 8 - b, 0), pltpu.roll(v, b, 0))
        return v

    @pl.loop(0, width // 16, unroll=4)
    def _(c):
        row = lax.broadcasted_iota(jnp.int32, (16, 128), 0) + 16 * c
        col = lax.broadcasted_iota(jnp.int32, (16, 128), 1)
        for t in range(nt):
            there = jnp.where(row == col * nt + t, 1.0, 0.0).astype(BF16)
            for part in range(3):
                at = pl.ds(pl.multiple_of(part * width + 16 * c, 16), 16)
                to_strided[at, t * 128 : (t + 1) * 128] = there

    weight = [(0.5 + l / lev) / lev for l in range(lev)]

    def columns(g):
        lo, hi = groups[g]
        view = vin.at[:, :, 8 * lo : 8 * hi, :]
        pltpu.make_async_copy(view, view, sem_in.at[g]).wait()

        @pl.loop(lo, hi)
        def _(c):
            row = pl.multiple_of(8 * c, 8)
            for t in range(lt):
                at = (pl.ds(row, 8), slice(t * 128, (t + 1) * 128))
                acc = [jnp.zeros((8, 128), F32)] * 3
                for l in range(lev):
                    p, h = weight[l] * vin[(0, l) + at], weight[l] * vin[(1, l) + at]
                    e, n = vin[(2, l) + at], vin[(3, l) + at]
                    acc = [acc[0] + p, acc[1] + (p * e + h * n), acc[2] + (p * n - h * e)]
                sig[t, pl.ds(row, 8), :] = acc[0]
                cur_e[t, pl.ds(row, 8), :] = acc[1]
                cur_n[t, pl.ds(row + 8, 8), :] = acc[2]

    def band(q):
        return slice(q * per * 8, (q + 1) * per * 8)

    def send_sig(q, recv):
        rcopy(sig.at[:, band(q)], sig_rx.at[:, band(q)], mirror, "sig", recv).start()

    def send_t(q, recv):
        rcopy(t_out.at[:, band(q)], t_rx.at[:, band(q)], mirror, "t", recv).start()

    def to_up(src_ref, dst_ref, recv):
        @pl.when(has_up)
        def _():
            rcopy(src_ref, dst_ref, up, "up", recv).start()

    def to_dn(src_ref, dst_ref, recv):
        @pl.when(has_dn)
        def _():
            rcopy(src_ref, dst_ref, dn, "dn", recv).start()

    def from_dn(name, view):
        @pl.when(has_dn)
        def _():
            arrived(name, view)

    def from_up(name, view):
        @pl.when(has_up)
        def _():
            arrived(name, view)

    def send_lon(slot, rx, g, recv):
        rcopy(pk.at[slot], rx.at[0, g], lf, "lon", recv).start()
        rcopy(pk.at[slot + 1], rx.at[1, g], rt, "lon", recv).start()

    for g in range(4):
        columns(g)
    pl.semaphore_wait(barrier, n_dev - 1)
    to_up(cur_n.at[:, 8:9], cur_n.at[:, rows + 8 : rows + 9], "n_up")
    to_dn(cur_n.at[:, rows + 7 : rows + 8], cur_n.at[:, 7:8], "n_dn")
    send_sig(0, "sig_a")
    send_sig(PIECES - 1, "sig_a")
    for q in range(1, PIECES - 1):
        columns(2 * q + 2)
        columns(2 * q + 3)
        if q != PIECES - 2:
            send_sig(q, "sig_b")

    step_e = 128 // n_rt
    pack(0, [cur_e[0, 8 * c : 8 * c + 8, :] for c in range(n_rt)], step_e, 0)
    pack(1, [cur_e[lt - 1, 8 * c : 8 * c + 8, :] for c in range(n_rt)], step_e, 1)
    send_lon(0, rx_e, 0, "e")

    outer, inner = [0, PIECES - 1], list(range(1, PIECES - 1))
    slot_s = 4
    slot_fars = slot_s + 2 * PIECES
    slot_v = slot_fars + 2 * len(inner)
    slot_in = slot_v + 2 * len(outer)
    slot_far = slot_in + 2
    slot_corner = slot_far + 2

    def two_terms(own, other, rx, slot, far, runs, edge, recv):
        for i, (lo, hi) in enumerate(runs):
            there = runs.index((n_rt - hi, n_rt - lo))
            for side, t in enumerate((0, lt - 1)):
                a, b = slot + 2 * i + side, far + 2 * i + side
                pack(a, [own[t, 8 * k : 8 * k + 8, :] for k in range(lo, hi)], edge, side * edge)
                pack(
                    b, [other[t, 8 * k : 8 * k + 8, :] for k in range(lo, hi)][::-1],
                    edge, side * edge,
                )
                rcopy(pk.at[a], rx.at[side, 0, i], (lf, rt)[side], "lon", recv).start()
                rcopy(pk.at[b], rx.at[side, 1, there], (far_lf, far_rt)[side], "lon", recv).start()

    two_terms(
        sig, sig, rx_ins, slot_s + 2 * len(outer), slot_fars,
        [(q * per, (q + 1) * per) for q in inner], EDGE, "inner_s",
    )

    @pl.when(jnp.logical_not(has_up))
    def _():
        cur_n[:, 0:8, :] = jnp.zeros((lt, 8, 128), F32)
        ion[:, :, 0:8, :] = jnp.zeros((3, lt, 8, 128), F32)
        S[:, 0:GUARD, :] = jnp.zeros((nt, GUARD, 128), F32)
        src[:, 0:GUARD, :] = jnp.zeros((nt, GUARD, 128), F32)

    @pl.when(jnp.logical_not(has_dn))
    def _():
        cur_n[:, rows + 8 : rows + 16, :] = jnp.zeros((lt, 8, 128), F32)
        ion[:, :, rows + 8 : rows + 16, :] = jnp.zeros((3, lt, 8, 128), F32)
        S[:, GUARD + rows :, :] = jnp.zeros((nt, GUARD, 128), F32)
        src[:, GUARD + rows :, :] = jnp.zeros((nt, GUARD, 128), F32)

    view = ion.at[:, :, 8 : 8 + rows]
    pltpu.make_async_copy(view, view, sem_ion.at[0]).wait()
    step_i = 128 // (3 * n_rt)
    bands = [(s, c) for s in range(3) for c in range(n_rt)]
    pack(2, [ion[s, 0, 8 * c + 8 : 8 * c + 16, :] for s, c in bands], step_i, 0)
    pack(3, [ion[s, lt - 1, 8 * c + 8 : 8 * c + 16, :] for s, c in bands], step_i, 1)
    send_lon(2, rx_ion, 0, "ion")

    from_dn("n_up", cur_n.at[:, 7:8])
    from_up("n_dn", cur_n.at[:, 7:8])
    arrived("e", rx_e)
    e_fr, e_fl = rx_e[0, 0, :, :], rx_e[1, 0, :, :]
    for q in [0, PIECES - 1] + list(range(1, PIECES - 1)):
        for c in range(q * per, (q + 1) * per):
            row = 8 * c
            at = slice(row, row + 8)
            left, right = shifts(
                [cur_e[t, at, :] for t in range(lt)],
                turn(e_fr, 127 - step_e * c), turn(e_fl, 128 - step_e * c),
            )
            for t in range(lt):
                d_lon = 0.5 * (right[t] - left[t])
                d_lat = 0.5 * (cur_n[t, row + 9 : row + 17, :] - cur_n[t, row + 7 : row + 15, :])
                s_one[t, at, :] = d_lon + d_lat
                t_out[t, at, :] = d_lon - d_lat
        if q in outer:
            send_t(q, "t_a")
    mid = (per, n_rt - per)
    edge_in = 128 // (mid[1] - mid[0])
    two_terms(s_one, t_out, rx_in, slot_in, slot_far, [mid], edge_in, "inner")

    for j in range(nt):
        @pl.loop(0, 8, unroll=2)
        def _(c):
            row = lax.broadcasted_iota(jnp.int32, (16, 128), 0) + 16 * c
            col = lax.broadcasted_iota(jnp.int32, (16, 128), 1)
            home = row * nt + j
            for t in range(lt):
                here = col + t * 128
                back = jnp.where(home == here, 1.0, 0.0).astype(BF16)
                before = jnp.where(here == 0, width - 1, here - 1)
                slope = jnp.where(
                    home == here + 1, 0.5, jnp.where(home == before, -0.5, 0.0)
                ).astype(BF16)
                for part in range(3):
                    at = pl.ds(pl.multiple_of(part * width + j * 128 + 16 * c, 16), 16)
                    to_plain[at, t * 128 : (t + 1) * 128] = back
                    to_plain[at, (lt + t) * 128 : (lt + t + 1) * 128] = slope

    def combine(own, rx, out, q):
        p = PIECES - 1 - q
        for c in range(p * per, (p + 1) * per):
            back = rows - 8 - 8 * c
            for t in range(lt):
                out[t, 8 * c + GUARD : 8 * c + GUARD + 8, :] = own[
                    t, 8 * c : 8 * c + 8, :
                ] + rev8(rx[t, back : back + 8, :])

    def spread(out, rx, slot, g, lo, count, recv):
        tiles = lambda t: [out[t, lo + 8 * k : lo + 8 * k + 8, :] for k in range(count)]
        pack(slot, tiles(0), EDGE, 0)
        pack(slot + 1, tiles(lt - 1), EDGE, EDGE)
        send_lon(slot, rx, g, recv)

    def unpack(out, fr, fl, lo, count, edge):
        for k in range(count):
            a, b = turn(fr, 128 - edge * k), turn(fl, 256 - edge - edge * k)
            out[lt, lo + 8 * k : lo + 8 * k + 8, :] = jnp.where(
                lane < edge, a, jnp.where(lane >= 128 - edge, b, 0.0)
            )

    def gather(out, rx, g, lo, count):
        unpack(out, rx[0, g, :, :], rx[1, g, :, :], lo, count, EDGE)

    def spread_piece(out, rx, slot, q, recv):
        p = PIECES - 1 - q
        spread(out, rx, slot, p, GUARD + p * per * 8, per, recv)

    def gather_piece(out, rx, q):
        p = PIECES - 1 - q
        gather(out, rx, p, GUARD + p * per * 8, per)

    def lat_send(out, rx, depth, name, slot):
        lo, hi = GUARD, GUARD + rows
        to_up(out.at[0:lt, lo : lo + depth], out.at[0:lt, hi : hi + depth], name + "_up")
        to_dn(out.at[0:lt, hi - depth : hi], out.at[0:lt, lo - depth : lo], name + "_dn")
        for edge, first in enumerate((lo, hi - depth)):
            for side, t in enumerate((0, lt - 1)):
                tiles = [out[t, r : r + 8, :] for r in range(first, first + depth, 8)]
                pack(slot + 2 * edge + side, tiles, EDGE, side * EDGE)

        def corners(edge, lat, send, recv):
            for side, lon in enumerate((lf[1], rt[1])):
                rcopy(
                    pk.at[slot + 2 * edge + side], rx.at[side, PIECES + 1 - edge], (lat, lon),
                    send, recv,
                ).start()

        @pl.when(has_up)
        def _():
            corners(0, up[0], "up_lon", name + "_hi")

        @pl.when(has_dn)
        def _():
            corners(1, dn[0], "dn_lon", name + "_lo")

    def lat_gather(out, rx, depth, name):
        lo, hi = GUARD, GUARD + rows

        @pl.when(has_up)
        def _():
            arrived(name + "_dn", out.at[0:lt, lo - depth : lo])
            arrived(name + "_lo", pk.at[0:2])
            gather(out, rx, PIECES, lo - depth, depth // 8)

        @pl.when(has_dn)
        def _():
            arrived(name + "_up", out.at[0:lt, lo - depth : lo])
            arrived(name + "_hi", pk.at[0:2])
            gather(out, rx, PIECES + 1, hi, depth // 8)

    arrived("ion", rx_ion)
    i_fr, i_fl = rx_ion[0, 0, :, :], rx_ion[1, 0, :, :]
    for k, (s, c) in enumerate(bands):
        at = slice(8 * c, 8 * c + 8)
        tiles = [ion[s, t, 8 * c + 8 : 8 * c + 16, :] for t in range(lt)]
        left, right = shifts(tiles, turn(i_fr, 127 - step_i * k), turn(i_fl, 128 - step_i * k))
        for t in range(lt):
            ion_a[s, t, at, :] = tiles[t] - left[t]
            ion_b[s, t, at, :] = right[t] - tiles[t]

    arrived("sig_a", sig_rx.at[:, 0 : 2 * per * 8])
    for q in outer:
        combine(sig, sig_rx, S, q)
    lat_send(S, rx_s, GUARD, "s", slot_corner)
    send_sig(PIECES - 2, "sig_b")
    for i, q in enumerate(outer):
        spread_piece(S, rx_s, slot_s + 2 * i, q, "s_lon")

    arrived("t_a", t_rx.at[:, 0 : 2 * per * 8])
    for q in outer:
        combine(s_one, t_rx, src, q)
    lat_send(src, rx_v, HALO, "v", slot_corner + 4)
    for q in inner:
        send_t(q, "t_b")
    to_up(ion.at[:, :, 8:9], ion.at[:, :, rows + 8 : rows + 9], "i_up")
    to_dn(ion.at[:, :, rows + 7 : rows + 8], ion.at[:, :, 7:8], "i_dn")
    for i, q in enumerate(outer):
        spread_piece(src, rx_v, slot_v + 2 * i, q, "v_lon")

    def inner_edges(out, pair, i, lo, count, edge):
        fr, fl = [pair[side, 0, i, :, :] + rev8(pair[side, 1, i, :, :]) for side in range(2)]
        unpack(out, fr, fl, GUARD + 8 * lo, count, edge)

    arrived("sig_b", sig_rx.at[:, 0 : (PIECES - 2) * per * 8])
    for q in inner:
        combine(sig, sig_rx, S, q)
    arrived("inner_s", rx_ins)
    for i, q in enumerate(inner):
        inner_edges(S, rx_ins, i, q * per, per, EDGE)
    arrived("s_lon", pk.at[0 : 2 * len(outer)])
    for q in outer:
        gather_piece(S, rx_s, q)
    lat_gather(S, rx_s, GUARD, "s")

    def split(v, at, t):
        for part in range(3):
            low = v.astype(BF16)
            lhs[at, part * width + t * 128 : part * width + (t + 1) * 128] = low
            v = v - low.astype(F32)

    def split_rows(ref, first, lo, hi):
        for row in range(lo, hi, 16):
            for t in range(nt):
                split(ref[t, row + first : row + first + 16, :], slice(row, row + 16), t)

    def conv_lon(v):
        after = v[1:] + [pltpu.roll(v[0], 127, 1)]
        p = [a + b for a, b in zip(v, after)]
        before = [pltpu.roll(p[-1], 1, 1)] + p[:-1]
        return [a + b for a, b in zip(p, before)]

    tall = rows + 2 * GUARD
    ext = rows + 2 * HALO
    split_rows(S, 0, 0, tall)
    moved = jnp.dot(lhs[0:tall, :], to_strided[...], preferred_element_type=F32)
    for t in range(nt):
        SP[t, :, :] = moved[:, t * 128 : (t + 1) * 128]

    for c in range(tall // 8):
        for t, v in enumerate(conv_lon([SP[t, 8 * c : 8 * c + 8, :] for t in range(nt)])):
            U[t, 8 * c : 8 * c + 8, :] = v

    total = rows * nlat
    skip = GUARD - HALO
    for c in range(R):
        where = sub * R + (c - HALO + me_lat * rows)
        inside = (where >= 0) & (where < total)
        at = slice(8 * c, 8 * c + 8)
        for t in range(nt):
            s = SP[t, pl.ds(skip + c, 8, stride=R), :]
            around = U[t, pl.ds(skip + c - 1, 8, stride=R), :] + U[
                t, pl.ds(skip + c + 1, 8, stride=R), :
            ]
            around = around + 2.0 * U[t, pl.ds(skip + c, 8, stride=R), :]
            inv = jnp.where(inside, 1.0 / (DAMPING + 2.0 * s + 0.25 * around), 0.0)
            quarter = 0.25 * inv
            SR[t, at, :] = s
            invR[t, at, :] = inv
            rR[t, at, :] = quarter
            mR[t, at, :] = (THETA - 1.0) - 8.0 * (quarter * s)
            X[1, t, at, :] = jnp.zeros((8, 128), F32)

    def transform(lo, hi):
        split_rows(src, skip, lo, hi)
        moved = jnp.dot(lhs[lo:hi, :], to_strided[...], preferred_element_type=F32)
        for t in range(nt):
            SP[t, lo:hi, :] = moved[:, t * 128 : (t + 1) * 128]

    arrived("v_lon", pk.at[0 : 2 * len(outer)])
    for q in outer:
        gather_piece(src, rx_v, q)
    lat_gather(src, rx_v, HALO, "v")
    late_lo, late_hi = HALO + 8 * mid[0], HALO + 8 * mid[1]
    transform(0, late_lo)
    transform(late_hi, ext)
    arrived("inner", rx_in)
    inner_edges(src, rx_in, 0, mid[0], mid[1] - mid[0], edge_in)
    arrived("t_b", t_rx.at[:, 0 : 8 * (mid[1] - mid[0])])
    for q in inner:
        combine(s_one, t_rx, src, q)
    transform(late_lo, late_hi)
    for c in range(R):
        at = slice(8 * c, 8 * c + 8)
        for t in range(nt):
            first = SP[t, pl.ds(c, 8, stride=R), :] * invR[t, at, :]
            spR[t, at, :] = first
            X[0, t, at, :] = first * (1.0 / THETA)

    def sweep(k, cur, prv, final):
        c1 = coef[0, k]
        c2 = coef[1, k]

        def smooth(c):
            at = slice(8 * c, 8 * c + 8)
            xs = [X[cur, t, at, :] for t in range(nt)]
            ys = [SR[t, at, :] * xs[t] for t in range(nt)]
            return xs, conv_lon(xs), conv_lon(ys)

        _, u_end, w_end = smooth(R - 1)
        xs, u, w = smooth(0)
        u_top, w_top = u, w
        qu = [pltpu.roll(a, 1, 0) + b for a, b in zip(u_end, u)]
        qw = [pltpu.roll(a, 1, 0) + b for a, b in zip(w_end, w)]
        for c in range(R):
            if c < R - 1:
                x_next, u_next, w_next = smooth(c + 1)
            else:
                x_next = None
                u_next = [pltpu.roll(v, 7, 0) for v in u_top]
                w_next = [pltpu.roll(v, 7, 0) for v in w_top]
            qu2 = [a + b for a, b in zip(u, u_next)]
            qw2 = [a + b for a, b in zip(w, w_next)]
            at = slice(8 * c, 8 * c + 8)
            for t in range(nt):
                pull = SR[t, at, :] * (qu[t] + qu2[t]) + (qw[t] + qw2[t])
                z = rR[t, at, :] * pull + (mR[t, at, :] * xs[t] + spR[t, at, :])
                new = c2 * z - c1 * X[prv, t, at, :]
                if final:
                    xr[t, pl.ds(8 + c, 8, stride=R), :] = new
                else:
                    X[prv, t, at, :] = new
            qu, qw, u, w, xs = qu2, qw2, u_next, w_next, x_next

    @pl.loop(0, (SWEEPS - 2) // 2)
    def _(k):
        sweep(2 * k, 0, 1, False)
        sweep(2 * k + 1, 1, 0, False)

    sweep(SWEEPS - 2, 0, 1, True)

    own0 = 8 + HALO
    best = jnp.zeros((8, 128), F32)
    for c in range(n_rt):
        lo = own0 + 8 * c
        x = [xr[t, lo : lo + 8, :] for t in range(nt)]
        after = x[1:] + [pltpu.roll(x[0], 127, 1)]
        before = [pltpu.roll(x[-1], 1, 1)] + x[:-1]
        for t in range(nt):
            speed = jnp.abs(0.5 * (xr[t, lo + 1 : lo + 9, :] - xr[t, lo - 1 : lo + 7, :]))
            speed = speed + jnp.abs(0.5 * (after[t] - before[t]))
            best = jnp.maximum(best, jnp.where(lane * nt + t < lt * 128, speed, 0.0))
    mx[0:1, :] = jnp.max(best, axis=0, keepdims=True)

    for o, dev in enumerate(others):
        rcopy(mx.at[0:1], mrx.at[o : o + 1], dev, "max", "max").start()

    near = rows + 16
    split_rows(xr, own0 - 8, 0, near)
    moved = jnp.dot(lhs[0:near, :], to_plain[...], preferred_element_type=F32)
    for t in range(lt):
        xn[t, :, :] = moved[:, t * 128 : (t + 1) * 128]
        dnb[t, :, :] = moved[:, (lt + t) * 128 : (lt + t + 1) * 128]
        pot_o[:, t * 128 : (t + 1) * 128] = moved[8 : 8 + rows, t * 128 : (t + 1) * 128]

    from_dn("i_up", ion.at[:, :, 7:8])
    from_up("i_dn", ion.at[:, :, 7:8])

    @pl.loop(0, n_rt, unroll=2)
    def _(c):
        row = pl.multiple_of(8 * c, 8)
        at = pl.ds(row, 8)
        for t in range(lt):
            de = -0.5 * (xn[t, pl.ds(row + 9, 8), :] - xn[t, pl.ds(row + 7, 8), :])
            dv = dnb[t, pl.ds(row + 8, 8), :]
            e_pos, e_neg = jnp.maximum(de, 0.0), jnp.minimum(de, 0.0)
            n_pos, n_neg = jnp.maximum(dv, 0.0), jnp.minimum(dv, 0.0)
            for s in range(3):
                n = ion[s, t, pl.ds(row + 8, 8), :]
                f = e_pos * ion_a[s, t, at, :] + e_neg * ion_b[s, t, at, :]
                f = f + n_pos * (n - ion[s, t, pl.ds(row + 7, 8), :])
                f = f + n_neg * (ion[s, t, pl.ds(row + 9, 8), :] - n)
                flux[s, t, at, :] = f

    arrived("max", mrx.at[0 : n_dev - 1])
    best = jnp.maximum(
        jnp.max(mrx[0 : n_dev - 1, :], axis=0, keepdims=True), mx[0:1, :]
    )
    best = jnp.max(best, axis=1, keepdims=True)
    step = jnp.broadcast_to(COURANT / (best + 1e-6), (8, 128))

    for s in range(3):
        scale = MOBILITY[s] * step

        @pl.loop(0, n_rt, unroll=2)
        def _(c):
            row = pl.multiple_of(8 * c, 8)
            for t in range(lt):
                upd_o[s, pl.ds(row, 8), t * 128 : (t + 1) * 128] = (
                    ion[s, t, pl.ds(row + 8, 8), :] - scale * flux[s, t, pl.ds(row, 8), :]
                )

    to_side = sig.at[:, 0 : 1 + 3 + GUARD + HALO]

    @pl.when(has_up)
    def _():
        sent("up", to_side)
        sent("up_lon", pk.at[0:4])

    @pl.when(has_dn)
    def _():
        sent("dn", to_side)
        sent("dn_lon", pk.at[0:4])

    sent("sig", sig)
    sent("t", t_out)
    sent("lon", pk.at[0:slot_corner])
    sent("max", mrx.at[0 : n_dev - 1])


def write_out(pot_v, upd_v, pot_h, upd_h, sem):
    copies = [pltpu.make_async_copy(upd_v.at[s], upd_h.at[s], sem.at[s]) for s in range(3)]
    copies.append(pltpu.make_async_copy(pot_v, pot_h, sem.at[3]))
    for c in copies:
        c.start()
    for c in copies:
        c.wait()


def solution(mesh):
    nlat, nlon = mesh.shape["lat"], mesh.shape["lon"]

    def shards(pedersen, hall_conductivity, east_wind, north_wind, ion_density):
        lev, rows, cols = pedersen.shape
        lt = cols // 128
        nt = lt + 1
        width = nt * 128
        tall = rows + 2 * GUARD
        ext = rows + 2 * HALO
        groups = PIECES + 2
        vm = lambda *shape: pltpu.VMEM(shape, F32)
        half = lambda *shape: pltpu.VMEM(shape, BF16)
        dma = lambda *shape: pltpu.SemaphoreType.DMA(shape)
        hbm = pl.BlockSpec(memory_space=pltpu.HBM)
        vmem = pl.BlockSpec(memory_space=pltpu.VMEM)
        pot, upd = pl.pallas_call(
            functools.partial(kernel, nlat, nlon, lev, rows, lt),
            out_shape=(pltpu.VMEM((rows, cols), F32), pltpu.VMEM((3, rows, cols), F32)),
            in_specs=[hbm] * 5,
            out_specs=(vmem, vmem),
            scratch_shapes=[vm(4, lev, rows, cols)]
            + [vm(3, lt, rows + 16, 128)] + [vm(3, lt, rows, 128)] * 2
            + [vm(lt, rows, 128), vm(lt, rows, 128), vm(lt, rows + 16, 128)]
            + [vm(lt, rows, 128)] * 4
            + [vm(nt, tall, 128)] * 2
            + [vm(8 * PIECES, 8, 128)] + [vm(2, 1, 8, 128)] * 2 + [vm(2, groups, 8, 128)] * 2
            + [vm(2, 2, 1, 8, 128), vm(2, 2, PIECES - 2, 8, 128)]
            + [half(tall, 3 * width), half(3 * width, width), half(3 * width, 2 * lt * 128)]
            + [pltpu.SMEM((2, SWEEPS), F32)]
            + [vm(nt, tall, 128)] * 2
            + [vm(nt, ext, 128)] * 5
            + [vm(2, nt, ext, 128), vm(nt, ext + 16, 128)]
            + [vm(lt, rows + 16, 128)] * 2
            + [vm(3, lt, rows, 128), vm(8, 128), vm(nlat * nlon, 128)]
            + [dma(len(in_groups(rows // 8))), dma(1), dma(len(SEND)), dma(len(RECV))],
            compiler_params=pltpu.CompilerParams(
                collective_id=0, has_side_effects=True, vmem_limit_bytes=60 * 1024 * 1024
            ),
        )(pedersen, hall_conductivity, east_wind, north_wind, ion_density)
        pot = pltpu.with_memory_space_constraint(pot, pltpu.VMEM)
        upd = pltpu.with_memory_space_constraint(upd, pltpu.VMEM)
        return pl.pallas_call(
            write_out,
            out_shape=(
                jax.ShapeDtypeStruct((rows, cols), F32),
                jax.ShapeDtypeStruct((3, rows, cols), F32),
            ),
            in_specs=[vmem, vmem],
            out_specs=(hbm, hbm),
            scratch_shapes=[dma(4)],
        )(pot, upd)

    spec = P(None, "lat", "lon")
    return jax.shard_map(
        shards,
        mesh=mesh,
        in_specs=(spec,) * 5,
        out_specs=(P("lat", "lon"), spec),
        check_vma=False,
    )
```
